32 devices in a mesh: grp: 2 (over y), sv: 4 (over z), tv: 4 (over x, core).
Axes of the slice: x: 2, y: 2, z: 4, core: 2. Of those that a mesh axis runs over, the one named last changes fastest.
Arguments:
- student_states: bfloat16 [512, 1792], P('grp', 'tv'), parts along dimension 0, may hold values from -60 to 60
- teacher_states: bfloat16 [512, 2304], P('grp', 'tv'), parts along dimension 0, may hold values from -60 to 60
- student_queries: bfloat16 [512, 256], P('grp', 'tv'), parts along dimension 0, may hold values from -60 to 60
- teacher_keys: bfloat16 [512, 256], P('grp', 'tv'), parts along dimension 0, may hold values from -6 to 6
- student_targets: int32 [512], P('grp'), parts along dimension 0, may hold values from 0 to 8191
- teacher_targets: int32 [512], P('grp'), parts along dimension 0, may hold values from 0 to 8191
- student_lengths: int32 [4], P('grp'), parts along dimension 0, may hold values from 64 to 128
- teacher_lengths: int32 [4], P('grp'), parts along dimension 0, may hold values from 64 to 128
- to_teacher: bfloat16 [1792, 2304], P('tv', 'sv'), may hold values from -0.125 to 0.125
- to_student: bfloat16 [2304, 1792], P('tv', 'sv'), may hold values from -0.125 to 0.125
- student_head: bfloat16 [1792, 8192], P(None, ('sv', 'tv')), may hold values from -0.125 to 0.125
- teacher_head: bfloat16 [2304, 8192], P(None, ('sv', 'tv')), may hold values from -0.125 to 0.125
Outputs:
- student_loss: float32 [512], P('grp'), parts along dimension 0
- teacher_loss: float32 [512], P('grp'), parts along dimension 0
- student_grad: bfloat16 [512, 8192], P('grp', ('sv', 'tv')), parts along dimension 0
- teacher_grad: bfloat16 [512, 8192], P('grp', ('sv', 'tv')), parts along dimension 0
The draws below stay inside these ranges and needn't reach their ends.
There are 2 independent parts, one for each index of `grp`. The reference program is written for one: setup_inputs(seed, part) draws one part's arguments, and reference() takes and returns one part's arrays. A program takes and returns all parts, laid end to end along the dimension named above; an argument that names none is the same for every part. Nothing has to cross between parts.
All inputs are finite; a program needn't handle non-finite values.
Results may differ from the reference program's by a relative error of at most 0.0086.
Values may be sent and summed in bfloat16 or wider, within the bound.
No kernel may reach another device: no remote copies, remote signals or barrier semaphores. Data moves between devices by JAX's collectives and lax.ppermute only.
A program may use at most 64 MiB of HBM per device.

```python
import math
import jax
import jax.numpy as jnp
import numpy as np
from jax import lax

DS = 1792
DT = 2304
DK = 256
LS = 128
SEQS = 2
LT = 128
ROWS = 256
TROWS = 256
VS = 8192
VT = 8192


def rough_rows(key, row_count, column_count):
    draw_values, draw_scales = jax.random.split(key, 2)
    entries = jnp.clip(jax.random.normal(draw_values, (row_count, column_count), jnp.float32), -4.0, 4.0)
    scales = jnp.exp(jax.random.uniform(draw_scales, (row_count, 1), jnp.float32, 0.0, 1.1))
    return scales * entries


def draw_student_states(key, part):
    return rough_rows(jax.random.fold_in(key, 11), ROWS, DS).astype(jnp.bfloat16)


def draw_teacher_states(key, part):
    return rough_rows(jax.random.fold_in(key, 23), TROWS, DT).astype(jnp.bfloat16)


def draw_student_queries(key, part):
    return rough_rows(jax.random.fold_in(key, 37), ROWS, DK).astype(jnp.bfloat16)


def touch_ends(drawn, rng, least, largest):
    longest = drawn.shape.index(max(drawn.shape))
    spots = []
    for shift in (0, 1):
        where = [jax.random.randint(jax.random.fold_in(rng, axis), (), 0, length) for axis, length in enumerate(drawn.shape)]
        where[longest] = (where[longest] + shift) % drawn.shape[longest]
        spots.append(tuple(where))
    return drawn.at[spots[0]].set(least).at[spots[1]].set(largest)


def steps_of(rng, dims, pieces, least, top_value):
    loudness = 1.0
    for dim, blocks in pieces:
        heights = jax.random.uniform(jax.random.fold_in(jax.random.fold_in(rng, 6), dim), (blocks,), jnp.float32, least / len(pieces), top_value / len(pieces))
        loudness = loudness * jnp.repeat(jnp.exp(heights), dims[dim] // blocks).reshape((-1,) + (1,) * (len(dims) - 1 - dim))
    return loudness


def rank_bounds(count, slope):
    portions = [(1 << 20) // math.isqrt(grade ** slope) + 1 for grade in range(1, count + 1)]
    spread = 1 + sum(portions) // (1 << 30)
    return np.cumsum(np.array([max(1, weight // spread) for weight in portions]))


def skewed_ids(stream_key, dims, count, slope):
    listing = rank_bounds(count, slope)
    pick = jax.random.randint(jax.random.fold_in(stream_key, 1), dims, 0, int(listing[count - 1]))
    grade = jnp.searchsorted(jnp.asarray(listing, jnp.int32), pick, side="right")
    return jax.random.permutation(jax.random.fold_in(stream_key, 2), count)[grade].astype(jnp.int32)


def scatter_about(key, dims, width, bound, cuts=(), held_as=jnp.bfloat16):
    values = width * jax.random.normal(key, dims, jnp.float32)
    if cuts:
        values = values * steps_of(key, dims, cuts, -0.22, 0.18)
    return jnp.clip(values, -bound, bound).astype(held_as)


def setup_inputs(seed: int = 0, part: int = 0) -> dict:
    key_list = jax.random.split(jax.random.key(seed), 13)
    part_keys = jax.random.split(jax.random.fold_in(key_list[12], part), 13)
    return {
        "student_states": draw_student_states(jax.random.fold_in(jax.random.fold_in(key_list[12], part), 71), part),
        "teacher_states": draw_teacher_states(jax.random.fold_in(jax.random.fold_in(key_list[12], part), 71), part),
        "student_queries": draw_student_queries(jax.random.fold_in(jax.random.fold_in(key_list[12], part), 71), part),
        "teacher_keys": scatter_about(part_keys[3], (TROWS, DK), 1.0, 6.0, ((1, 4),)),
        "student_targets": touch_ends(skewed_ids(part_keys[4], (ROWS,), VS, 2), jax.random.fold_in(part_keys[4], 3), 0, VS - 1).astype(jnp.int32),
        "teacher_targets": touch_ends(skewed_ids(part_keys[5], (ROWS,), VT, 2), jax.random.fold_in(part_keys[5], 3), 0, VT - 1).astype(jnp.int32),
        "student_lengths": jax.random.randint(part_keys[6], (SEQS,), LS // 2, LS + 1).astype(jnp.int32),
        "teacher_lengths": jax.random.randint(part_keys[7], (SEQS,), LT // 2, LT + 1).astype(jnp.int32),
        "to_teacher": scatter_about(key_list[8], (DS, DT), DS ** -0.5, 0.125, ((0, 4), (1, 4))),
        "to_student": scatter_about(key_list[9], (DT, DS), DT ** -0.5, 0.125, ((0, 4), (1, 4))),
        "student_head": scatter_about(key_list[10], (DS, VS), DS ** -0.5, 0.125, ((1, 16),)),
        "teacher_head": scatter_about(key_list[11], (DT, VT), DT ** -0.5, 0.125, ((1, 16),)),
    }


floor_value = -1.0e30


def align_rows(student_queries, teacher_keys, teacher_states, teacher_lengths):
    sequences = teacher_lengths.shape[0]
    key_width = student_queries.shape[1]
    queries = student_queries.astype(jnp.float32).reshape(sequences, -1, key_width)
    keyset = teacher_keys.astype(jnp.float32).reshape(sequences, -1, key_width)
    scores = jnp.einsum("sid,sjd->sij", queries, keyset, precision=lax.Precision.HIGHEST) * (key_width ** -0.5)
    positions = lax.broadcasted_iota(jnp.int32, scores.shape, 2)
    scores = jnp.where(positions < teacher_lengths[:, None, None], scores, floor_value)
    highest = jnp.max(scores, axis=2, keepdims=True)
    weights = jnp.exp(scores - highest)
    weights = lax.optimization_barrier((weights / jnp.sum(weights, axis=2, keepdims=True)).astype(jnp.bfloat16))
    states = teacher_states.astype(jnp.float32).reshape(sequences, -1, teacher_states.shape[1])
    aligned = jnp.einsum("sij,sjd->sid", weights.astype(jnp.float32), states, precision=lax.Precision.HIGHEST)
    return aligned.astype(jnp.bfloat16).reshape(-1, teacher_states.shape[1])


def live_rows(row_start, row_count, lengths, sequence_length):
    indices = row_start + lax.broadcasted_iota(jnp.int32, (row_count,), 0)
    sequence = indices // sequence_length
    position = indices % sequence_length
    owners = lax.broadcasted_iota(jnp.int32, (row_count, lengths.shape[0]), 1)
    length_limit = jnp.sum(jnp.where(sequence[:, None] == owners, lengths[None, :], 0), axis=1)
    return (position < length_limit).astype(jnp.float32)


def log_total(logits):
    highest = jnp.max(logits, axis=1, keepdims=True)
    return highest[:, 0] + jnp.log(jnp.sum(jnp.exp(logits - highest), axis=1))


def one_hot(targets, vocab_size):
    column = lax.broadcasted_iota(jnp.int32, (targets.shape[0], vocab_size), 1)
    return (column == targets[:, None]).astype(jnp.float32)


def picked_at(logits, targets):
    return jnp.take_along_axis(logits, targets[:, None].astype(jnp.int32), axis=1)[:, 0]


def reference(student_states, teacher_states, student_queries, teacher_keys, student_targets, teacher_targets, student_lengths, teacher_lengths, to_teacher, to_student, student_head, teacher_head):
    aligned = align_rows(student_queries, teacher_keys, teacher_states, teacher_lengths)
    into_teacher = jnp.dot(student_states, to_teacher, preferred_element_type=jnp.float32).astype(jnp.bfloat16)
    into_student = jnp.dot(aligned, to_student, preferred_element_type=jnp.float32).astype(jnp.bfloat16)
    student_own = jnp.dot(student_states, student_head, preferred_element_type=jnp.float32)
    student_mapped = jnp.dot(into_student, student_head, preferred_element_type=jnp.float32)
    teacher_own = jnp.dot(aligned, teacher_head, preferred_element_type=jnp.float32)
    teacher_mapped = jnp.dot(into_teacher, teacher_head, preferred_element_type=jnp.float32)
    row_total = student_states.shape[0]
    live_mask = live_rows(0, row_total, student_lengths, row_total // student_lengths.shape[0])

    own_total = log_total(student_own)
    mapped_total = log_total(student_mapped)
    own_chance = jnp.exp(student_own - own_total[:, None])
    mapped_chance = jnp.exp(student_mapped - mapped_total[:, None])
    student_diverge = jnp.sum(mapped_chance * (student_mapped - student_own), axis=1) - mapped_total + own_total
    student_loss = live_mask * (own_total - picked_at(student_own, student_targets) + mapped_total - picked_at(student_mapped, student_targets) + student_diverge)
    student_grad = (live_mask[:, None] * (2.0 * own_chance - one_hot(student_targets, student_own.shape[1]) - mapped_chance)).astype(jnp.bfloat16)

    teacher_total = log_total(teacher_own)
    projected_total = log_total(teacher_mapped)
    teacher_chance = jnp.exp(teacher_own - teacher_total[:, None])
    projected_chance = jnp.exp(teacher_mapped - projected_total[:, None])
    teacher_diverge = jnp.sum(teacher_chance * (teacher_own - teacher_mapped), axis=1) - teacher_total + projected_total
    teacher_loss = live_mask * (teacher_diverge + projected_total - picked_at(teacher_mapped, teacher_targets))
    teacher_grad = (live_mask[:, None] * (2.0 * projected_chance - teacher_chance - one_hot(teacher_targets, teacher_own.shape[1]))).astype(jnp.bfloat16)
    return student_loss, teacher_loss, student_grad, teacher_grad
```

```python
import functools

import jax
import jax.numpy as jnp
from jax import lax
from jax.experimental import pallas as pl
from jax.experimental.pallas import tpu as pltpu
from jax.sharding import PartitionSpec as P

DK = 256
FLOOR = -1e30
CORES = 2
STATS = 8
F32 = jnp.float32
BF16 = jnp.bfloat16

VMEM = pl.BlockSpec(memory_space=pltpu.VMEM)
SMEM = pl.BlockSpec(memory_space=pltpu.SMEM)


def kernel_call(body, out_shape, in_specs, scratch=(), cost=1_000_000):
    single = not isinstance(out_shape, (tuple, list))
    return pl.pallas_call(
        body,
        out_shape=out_shape,
        in_specs=in_specs,
        out_specs=VMEM if single else [VMEM] * len(out_shape),
        scratch_shapes=list(scratch),
        compiler_params=pltpu.CompilerParams(vmem_limit_bytes=48 * 2**20),
        cost_estimate=pl.CostEstimate(flops=cost, bytes_accessed=cost, transcendentals=0),
    )


def dot00(a, b):
    return lax.dot_general(a, b, (((0,), (0,)), ((), ())), preferred_element_type=F32)


def dot10(a, b):
    return lax.dot_general(a, b, (((1,), (0,)), ((), ())), preferred_element_type=F32)


def half(core, width):
    return pl.ds(pl.multiple_of(core * width, width), width)


def project_teacher(core_ref, own_s, mate_s, own_w, mate_w, out_ref):
    cols = half(core_ref[0], out_ref.shape[1])
    out_ref[...] = dot00(own_w[...], own_s[:, cols]) + dot00(mate_w[...], mate_s[:, cols])


def attend(core_ref, lens_ref, q_ref, k_ref, own_t, mate_t, own_w, mate_w, out_ref, weights_ref):
    sequences = lens_ref.shape[0]
    width = q_ref.shape[1] // sequences
    for s in range(sequences):
        tokens = slice(s * width, (s + 1) * width)
        scores = dot00(k_ref[:, tokens], q_ref[:, tokens]) * DK ** (-0.5)
        position = lax.broadcasted_iota(jnp.int32, scores.shape, 0)
        scores = jnp.where(position < lens_ref[s], scores, FLOOR)
        raised = jnp.exp(scores - jnp.max(scores, axis=0, keepdims=True))
        weights_ref[s] = (raised / jnp.sum(raised, axis=0, keepdims=True)).astype(BF16)
    per_core = sequences // CORES
    for n in range(per_core):
        s = core_ref[0] * per_core + n
        weights = weights_ref[s]
        tokens = half(s, width)
        own = dot10(own_t[:, tokens], weights).astype(BF16)
        mate = dot10(mate_t[:, tokens], weights).astype(BF16)
        out_ref[:, n * width : (n + 1) * width] = dot10(own_w[...], own) + dot10(mate_w[...], mate)


def own_logits(blocks, index_ref, weights_ref, *refs):
    s_refs, t_refs = refs[:blocks], refs[blocks : 2 * blocks]
    s_head, t_head, s_out, t_out, s_all, t_all = refs[2 * blocks :]
    sequences, width, _ = weights_ref.shape
    s_rows, t_rows = s_refs[0].shape[0], t_refs[0].shape[0]
    for n in range(blocks):
        index = index_ref[n]
        s_all[half(index, s_rows), :] = s_refs[n][...]
        for s in range(sequences):
            tokens = slice(s * width, (s + 1) * width)
            t_all[half(index, t_rows), tokens] = dot10(t_refs[n][:, tokens], weights_ref[s]).astype(BF16)
    s_out[...] = dot00(s_all[...], s_head[...])
    t_out[...] = dot00(t_all[...], t_head[...])


def local_side(own, mapped, columns, forward, pick_both):
    def total(logits):
        highest = jnp.max(logits, axis=1, keepdims=True)
        raised = jnp.exp(logits - highest)
        summed = jnp.sum(raised, axis=1, keepdims=True)
        return raised, summed, highest + jnp.log(summed)

    own_raised, own_sum, own_total = total(own)
    mapped_raised, mapped_sum, mapped_total = total(mapped)
    if forward == "mapped":
        spread = jnp.sum(mapped_raised * (mapped - own), axis=1, keepdims=True) / mapped_sum
    else:
        spread = jnp.sum(own_raised * (own - mapped), axis=1, keepdims=True) / own_sum
    lane = lax.broadcasted_iota(jnp.int32, own.shape, 1)
    picked = own + mapped if pick_both else mapped
    picked = jnp.sum(jnp.where(lane == columns, picked, 0.0), axis=1, keepdims=True)
    return own_total, mapped_total, spread, picked


def target_columns(refs, base):
    row = lax.broadcasted_iota(jnp.int32, (STATS, refs[0].shape[1]), 0)
    stacked = jnp.where(row == 0, refs[0][...] - base, refs[1][...] - base).astype(F32)
    turned = jnp.transpose(stacked)
    return turned[:, 0:1].astype(jnp.int32), turned[:, 1:2].astype(jnp.int32)


def mapped_logits(blocks, index_ref, s_targets, t_targets, s_own, t_own, *refs):
    s_refs, t_refs = refs[: 2 * blocks], refs[2 * blocks : 4 * blocks]
    s_head, t_head, s_out, t_out, stats_out, s_all, t_all = refs[4 * blocks :]
    core, base = index_ref[blocks], index_ref[blocks + 1]
    width = s_refs[0].shape[1]
    for n in range(blocks):
        index = index_ref[n]
        for side in range(CORES):
            tokens = half(core if side == 0 else 1 - core, width)
            s_all[half(index, s_refs[0].shape[0]), tokens] = s_refs[2 * n + side][...]
            t_all[half(index, t_refs[0].shape[0]), tokens] = t_refs[2 * n + side][...]
    s_mapped = dot00(s_all[...], s_head[...])
    s_out[...] = s_mapped
    t_mapped = dot00(t_all[...], t_head[...])
    t_out[...] = t_mapped
    s_columns, t_columns = target_columns((s_targets, t_targets), base)
    so, sm, s_spread, s_picked = local_side(s_own[...], s_mapped, s_columns, "mapped", True)
    to, tm, t_spread, t_picked = local_side(t_own[...], t_mapped, t_columns, "own", False)
    lane = lax.broadcasted_iota(jnp.int32, (so.shape[0], 128), 1)
    packed = jnp.zeros(lane.shape, F32)
    for k, column in enumerate((so, sm, to, tm, s_spread, s_picked, t_spread, t_picked)):
        packed = jnp.where(lane == k, column, packed)
    stats_out[...] = jnp.transpose(packed)[:STATS]


def merge_stats(parts):
    highest = parts[0]
    for part in parts[1:]:
        highest = jnp.maximum(highest, part)
    scales = [jnp.exp(part - highest) for part in parts]
    total = highest + jnp.log(sum(scales))
    shares = [jnp.exp(part - total) for part in parts]
    s_spread = sum(share[1:2] * part[4:5] for share, part in zip(shares, parts))
    t_spread = sum(share[2:3] * part[6:7] for share, part in zip(shares, parts))
    s_picked = sum(part[5:6] for part in parts)
    t_picked = sum(part[7:8] for part in parts)
    return total, s_spread, s_picked, t_spread, t_picked


def merge_kernel(parts, in_ref, out_ref):
    total, *rest = merge_stats([in_ref[n * STATS : (n + 1) * STATS, :] for n in range(parts)])
    row = lax.broadcasted_iota(jnp.int32, total.shape, 0)
    for k, value in enumerate(rest):
        total = jnp.where(row == 4 + k, value, total)
    out_ref[...] = total


def finish(parts, index_ref, lens_ref, s_targets, t_targets, so_ref, sm_ref, to_ref, tm_ref, *refs):
    s_loss, t_loss, s_grad, t_grad = refs[parts:]
    totals, s_spread, s_picked, t_spread, t_picked = merge_stats([ref[...] for ref in refs[:parts]])
    so, sm, to, tm = (totals[k : k + 1] for k in range(4))
    rows = s_loss.shape[1]
    sequences = lens_ref.shape[0]
    width = rows // sequences

    def live(shape, dim):
        place = lax.broadcasted_iota(jnp.int32, shape, dim)
        mask = jnp.zeros(shape, jnp.bool_)
        for s in range(sequences):
            mask |= (place >= s * width) & (place < s * width + lens_ref[s])
        return mask.astype(F32)

    live_row = live((1, rows), 1)
    s_loss[...] = live_row * (so + sm - s_picked + (s_spread - sm + so))
    t_loss[...] = live_row * ((t_spread - to + tm) + tm - t_picked)
    turned = jnp.transpose(totals)
    live_column = live((rows, 1), 0)
    s_columns, t_columns = target_columns((s_targets, t_targets), index_ref[0])
    lane = lax.broadcasted_iota(jnp.int32, so_ref.shape, 1)
    s_hot = (lane == s_columns).astype(F32)
    t_hot = (lane == t_columns).astype(F32)
    so_chance = jnp.exp(so_ref[...] - turned[:, 0:1])
    sm_chance = jnp.exp(sm_ref[...] - turned[:, 1:2])
    to_chance = jnp.exp(to_ref[...] - turned[:, 2:3])
    tm_chance = jnp.exp(tm_ref[...] - turned[:, 3:4])
    s_grad[...] = (live_column * (2.0 * so_chance - s_hot - sm_chance)).astype(BF16)
    t_grad[...] = (live_column * (2.0 * tm_chance - to_chance - t_hot)).astype(BF16)


def body(
    student_states,
    teacher_states,
    student_queries,
    teacher_keys,
    student_targets,
    teacher_targets,
    student_lengths,
    teacher_lengths,
    to_teacher,
    to_student,
    student_head,
    teacher_head,
):
    rows = student_states.shape[0]
    tv_count, sv_count = lax.axis_size("tv"), lax.axis_size("sv")
    chips = tv_count // CORES
    tv, sv = lax.axis_index("tv"), lax.axis_index("sv")
    core = tv % CORES
    vocab = student_head.shape[1]
    base = (sv * tv_count + tv) * vocab

    def swap(a):
        return lax.ppermute(a, "tv", [(t, t ^ 1) for t in range(tv_count)])

    def across(a):
        return [
            lax.ppermute(a, "tv", [(t, (t + CORES * n) % tv_count) for t in range(tv_count)])
            for n in range(1, chips)
        ]

    def along(a):
        return [
            lax.ppermute(a, "sv", [(z, (z + n) % sv_count) for z in range(sv_count)])
            for n in range(1, sv_count)
        ]

    s_t, t_t = student_states.T, teacher_states.T
    w_t, w_s = to_teacher, to_student.T
    core_index = core.astype(jnp.int32).reshape(1)

    mate_w_t, mate_s = swap(w_t), swap(s_t)
    mate_t, mate_w_s = swap(t_t), swap(w_s)
    tokens = rows // CORES
    part_t = kernel_call(
        project_teacher,
        jax.ShapeDtypeStruct((w_t.shape[1], tokens), F32),
        [SMEM] + [VMEM] * 4,
    )(core_index, s_t, mate_s, w_t, mate_w_t)
    other_t = across(part_t)

    queries = lax.all_gather(student_queries.T, "tv", axis=0, tiled=True)
    keys = lax.all_gather(teacher_keys.T, "tv", axis=0, tiled=True)
    sequences = teacher_lengths.shape[0]
    width = rows // sequences
    part_s, weights = kernel_call(
        attend,
        (
            jax.ShapeDtypeStruct((w_s.shape[0], tokens), F32),
            jax.ShapeDtypeStruct((sequences, width, width), BF16),
        ),
        [SMEM] * 2 + [VMEM] * 6,
    )(core_index, teacher_lengths, queries, keys, t_t, mate_t, w_s, mate_w_s)
    other_s = across(part_s)

    into_t = functools.reduce(jnp.add, other_t, part_t).astype(BF16)
    into_t = [into_t] + along(into_t)
    into_s = functools.reduce(jnp.add, other_s, part_s).astype(BF16)
    into_s = [into_s] + along(into_s)

    far_s, far_t = across(s_t), across(t_t)
    s_blocks, t_blocks = [s_t, mate_s], [t_t, mate_t]
    for a, b in zip(far_s, far_t):
        s_blocks += [a, swap(a)]
        t_blocks += [b, swap(b)]
    own_index = []
    for n in range(chips):
        source = (tv - CORES * n) % tv_count
        own_index += [source, source ^ 1]
    own_index = jnp.stack(own_index).astype(jnp.int32)
    logits = jax.ShapeDtypeStruct((rows, vocab), F32)
    s_own, t_own = kernel_call(
        functools.partial(own_logits, tv_count),
        (logits, logits),
        [SMEM] + [VMEM] * (1 + 2 * tv_count + 2),
        [
            pltpu.VMEM((student_head.shape[0], rows), BF16),
            pltpu.VMEM((teacher_head.shape[0], rows), BF16),
        ],
    )(own_index, weights, *s_blocks, *t_blocks, student_head, teacher_head)

    s_pieces = [p for a in into_s for p in (a, swap(a))]
    t_pieces = [p for a in into_t for p in (a, swap(a))]
    mapped_index = jnp.stack(
        [(sv - n) % sv_count for n in range(sv_count)] + [core, base]
    ).astype(jnp.int32)
    s_targets, t_targets = student_targets.reshape(1, rows), teacher_targets.reshape(1, rows)
    s_mapped, t_mapped, stats = kernel_call(
        functools.partial(mapped_logits, sv_count),
        (logits, logits, jax.ShapeDtypeStruct((STATS, rows), F32)),
        [SMEM] + [VMEM] * (4 + 4 * sv_count + 2),
        [
            pltpu.VMEM((student_head.shape[0], rows), BF16),
            pltpu.VMEM((teacher_head.shape[0], rows), BF16),
        ],
    )(mapped_index, s_targets, t_targets, s_own, t_own, *s_pieces, *t_pieces, student_head, teacher_head)

    stats = lax.all_gather(stats, "tv", axis=0, tiled=True)
    stats = kernel_call(
        functools.partial(merge_kernel, tv_count),
        jax.ShapeDtypeStruct((STATS, rows), F32),
        [VMEM],
    )(stats)
    stats = [stats] + along(stats)
    loss = jax.ShapeDtypeStruct((1, rows), F32)
    grad = jax.ShapeDtypeStruct((rows, vocab), BF16)
    s_loss, t_loss, s_grad, t_grad = kernel_call(
        functools.partial(finish, sv_count),
        (loss, loss, grad, grad),
        [SMEM] * 2 + [VMEM] * (6 + sv_count),
    )(
        base.astype(jnp.int32).reshape(1),
        student_lengths,
        s_targets,
        t_targets,
        s_own,
        s_mapped,
        t_own,
        t_mapped,
        *stats,
    )
    return s_loss.reshape(rows), t_loss.reshape(rows), s_grad, t_grad


def solution(mesh):
    in_specs = (
        P("grp", "tv"),
        P("grp", "tv"),
        P("grp", "tv"),
        P("grp", "tv"),
        P("grp"),
        P("grp"),
        P("grp"),
        P("grp"),
        P("tv", "sv"),
        P("tv", "sv"),
        P(None, ("sv", "tv")),
        P(None, ("sv", "tv")),
    )
    out_specs = (P("grp"), P("grp"), P("grp", ("sv", "tv")), P("grp", ("sv", "tv")))
    return jax.shard_map(body, mesh=mesh, in_specs=in_specs, out_specs=out_specs, check_vma=False)
```

```python
import functools

import jax
import jax.numpy as jnp
from jax import lax
from jax.experimental import pallas as pl
from jax.experimental.pallas import tpu as pltpu
from jax.sharding import PartitionSpec as P

DK = 256
FLOOR = -1e30
CORES = 2
STATS = 8
F32 = jnp.float32
BF16 = jnp.bfloat16

VMEM = pl.BlockSpec(memory_space=pltpu.VMEM)
SMEM = pl.BlockSpec(memory_space=pltpu.SMEM)
HBM = pl.BlockSpec(memory_space=pltpu.HBM)


def shape(dims, dtype=F32):
    return jax.ShapeDtypeStruct(dims, dtype)


def kernel_call(body, out_shape, in_specs, scratch=(), limit=32):
    single = not isinstance(out_shape, (tuple, list))
    return pl.pallas_call(
        body,
        out_shape=out_shape,
        in_specs=in_specs,
        out_specs=VMEM if single else [VMEM] * len(out_shape),
        scratch_shapes=list(scratch),
        compiler_params=pltpu.CompilerParams(vmem_limit_bytes=limit * 2**20),

    )


def dot00(a, b):
    return lax.dot_general(a, b, (((0,), (0,)), ((), ())), preferred_element_type=F32)


def dot10(a, b):
    return lax.dot_general(a, b, (((1,), (0,)), ((), ())), preferred_element_type=F32)


def part_of(index, width):
    return pl.ds(pl.multiple_of(index * width, width), width)


def behind(axis, offset):
    count = lax.axis_size(axis)
    return lax.rem(lax.axis_index(axis) - offset + count, count)


def vocab_base(vocab):
    place = lax.axis_index("sv") * lax.axis_size("x") + lax.axis_index("x")
    return (place * CORES + lax.axis_index("core")) * vocab


def fetch(sems, *pairs):
    copies = [pltpu.make_async_copy(a, b, sems.at[n]) for n, (a, b) in enumerate(pairs)]
    for copy in copies:
        copy.start()
    return copies


def pack_kernel(q_ref, k_ref, out_ref, sems):
    rows = q_ref.shape[0]
    for copy in fetch(sems, (q_ref, out_ref.at[:rows]), (k_ref, out_ref.at[rows:])):
        copy.wait()


def project(states, matrix, *out_refs):
    *shares, total = out_refs
    total[...] = dot00(matrix[...], states[:, part_of(lax.axis_index("core"), total.shape[1])])
    rows = shares[0].shape[0]
    for n, share in enumerate(shares):
        share[...] = total[part_of(behind("x", lax.axis_size("x") - n), rows), :]


def collect(axis, *refs):
    *blocks, out_ref = refs
    rows = blocks[0].shape[0]
    for n, block in enumerate(blocks):
        out_ref[part_of(behind(axis, n), rows), :] = block[...]


def attend(blocks, lens_ref, states, matrix, *refs):
    qk_refs = refs[:blocks]
    out_ref, weights_ref, q_all, k_all = refs[blocks:]
    rows = qk_refs[0].shape[0] // 2
    for n, ref in enumerate(qk_refs):
        q_all[n * rows : (n + 1) * rows, :] = ref[:rows]
        k_all[n * rows : (n + 1) * rows, :] = ref[rows:]
    sequences = lens_ref.shape[0]
    width = q_all.shape[1] // sequences
    for s in range(sequences):
        tokens = slice(s * width, (s + 1) * width)
        scores = dot00(k_all[:, tokens], q_all[:, tokens]) * DK ** (-0.5)
        position = lax.broadcasted_iota(jnp.int32, scores.shape, 0)
        scores = jnp.where(position < lens_ref[s], scores, FLOOR)
        raised = jnp.exp(scores - jnp.max(scores, axis=0, keepdims=True))
        weights_ref[s] = (raised / jnp.sum(raised, axis=0, keepdims=True)).astype(BF16)
    per_core = sequences // CORES
    rows, cols = states.shape[0] // CORES, out_ref.shape[0]
    for n in range(per_core):
        s = lax.axis_index("core") * per_core + n
        aligned = dot10(states[:, part_of(s, width)], weights_ref[s]).astype(BF16)
        total = sum(
            dot10(matrix[c * cols : (c + 1) * cols, :], aligned[c * rows : (c + 1) * rows])
            for c in range(CORES)
        )
        out_ref[:, n * width : (n + 1) * width] = total


def log_total(logits):
    highest = jnp.max(logits, axis=1, keepdims=True)
    raised = jnp.exp(logits - highest)
    summed = jnp.sum(raised, axis=1, keepdims=True)
    return raised, summed, highest + jnp.log(summed)


def target_column(ref, base):
    row = jnp.broadcast_to((ref[...] - base).astype(F32), (STATS, ref.shape[1]))
    return jnp.transpose(row)[:, 0:1].astype(jnp.int32)


def pick(logits, columns):
    lane = lax.broadcasted_iota(jnp.int32, logits.shape, 1)
    return jnp.sum(jnp.where(lane == columns, logits, 0.0), axis=1, keepdims=True)


def pack_columns(columns):
    lane = lax.broadcasted_iota(jnp.int32, (columns[0].shape[0], 128), 1)
    packed = jnp.zeros(lane.shape, F32)
    for k, column in enumerate(columns):
        packed = jnp.where(lane == k, column, packed)
    return packed


def own_student(targets, *refs):
    *blocks, head, out_ref, notes_ref, s_all = refs
    collect("x", *blocks, s_all)
    logits = dot00(s_all[...], head[...])
    out_ref[...] = logits
    columns = target_column(targets, vocab_base(head.shape[1]))
    _, _, total = log_total(logits)
    notes_ref[...] = pack_columns((total, pick(logits, columns)))


def own_teacher(weights_ref, *refs):
    *blocks, head, own_ref, t_all = refs
    sequences, width, _ = weights_ref.shape
    rows = blocks[0].shape[0]
    for n, block in enumerate(blocks):
        for s in range(sequences):
            tokens = slice(s * width, (s + 1) * width)
            aligned = dot10(block[:, tokens], weights_ref[s]).astype(BF16)
            t_all[part_of(behind("x", n), rows), tokens] = aligned
    own_ref[...] = dot00(t_all[...], head[...])


def mapped_teacher(targets, own_ref, *refs):
    *shares, head, mapped_ref, stats_ref, t_all = refs
    parts, blocks = len(shares), lax.axis_size("sv")
    width = shares[0].shape[1]
    rows = shares[0].shape[0] // (CORES * blocks)
    for n, share in enumerate(shares):
        part = behind("x", n) if parts > 1 else 0
        for c in range(CORES):
            tokens = slice(c * width, (c + 1) * width)
            for z in range(blocks):
                place = (c * blocks + z) * rows
                t_all[part_of(z * parts + part, rows), tokens] = share[place : place + rows, :]
    mapped = dot00(t_all[...], head[...])
    mapped_ref[...] = mapped
    own = own_ref[...]
    columns = target_column(targets, vocab_base(head.shape[1]))
    raised, summed, own_total = log_total(own)
    _, _, mapped_total = log_total(mapped)
    spread = jnp.sum(raised * (own - mapped), axis=1, keepdims=True) / summed
    zero = jnp.zeros_like(spread)
    columns = (zero, zero, own_total, mapped_total, zero, zero, spread, pick(mapped, columns))
    stats_ref[...] = jnp.transpose(pack_columns(columns))[:STATS]


def student_side(targets, t_stats, own_ref, notes_ref, halves, head, mapped_ref, stats_ref):
    rows = halves.shape[0] // CORES
    states = jnp.concatenate([halves[:rows], halves[rows:]], axis=1)
    mapped = dot00(states, head[...])
    mapped_ref[...] = mapped
    columns = target_column(targets, vocab_base(head.shape[1]))
    raised, summed, total = log_total(mapped)
    spread = jnp.sum(raised * (mapped - own_ref[...]), axis=1, keepdims=True) / summed
    zero = jnp.zeros_like(spread)
    picked = notes_ref[:, 1:2] + pick(mapped, columns)
    columns = (notes_ref[:, 0:1], total, zero, zero, spread, picked)
    stats_ref[...] = jnp.transpose(pack_columns(columns))[:STATS] + t_stats[...]


def merge_stats(parts):
    highest = parts[0]
    for part in parts[1:]:
        highest = jnp.maximum(highest, part)
    total = highest + jnp.log(sum(jnp.exp(part - highest) for part in parts))
    shares = [jnp.exp(part - total) for part in parts]
    s_spread = sum(share[1:2] * part[4:5] for share, part in zip(shares, parts))
    s_picked = sum(part[5:6] for part in parts)
    t_spread = sum(share[2:3] * part[6:7] for share, part in zip(shares, parts))
    t_picked = sum(part[7:8] for part in parts)
    return total, s_spread, s_picked, t_spread, t_picked


def merge_kernel(parts, in_ref, out_ref):
    total, *rest = merge_stats([in_ref[n * STATS : (n + 1) * STATS, :] for n in range(parts)])
    row = lax.broadcasted_iota(jnp.int32, total.shape, 0)
    for k, value in enumerate(rest):
        total = jnp.where(row == 4 + k, value, total)
    out_ref[...] = total


def finish(parts, lens_ref, s_targets, t_targets, so_ref, sm_ref, to_ref, tm_ref, *refs):
    s_loss, t_loss, s_grad, t_grad = refs[parts:]
    totals, s_spread, s_picked, t_spread, t_picked = merge_stats([ref[...] for ref in refs[:parts]])
    so, sm, to, tm = (totals[k : k + 1] for k in range(4))
    rows = s_loss.shape[1]
    sequences = lens_ref.shape[0]
    width = rows // sequences

    def live(dims, dim):
        place = lax.broadcasted_iota(jnp.int32, dims, dim)
        mask = jnp.zeros(dims, jnp.bool_)
        for s in range(sequences):
            mask |= (place >= s * width) & (place < s * width + lens_ref[s])
        return mask.astype(F32)

    live_row = live((1, rows), 1)
    s_loss[...] = live_row * (so + sm - s_picked + (s_spread - sm + so))
    t_loss[...] = live_row * ((t_spread - to + tm) + tm - t_picked)
    turned = jnp.transpose(totals)
    live_column = live((rows, 1), 0)
    base = vocab_base(so_ref.shape[1])
    lane = lax.broadcasted_iota(jnp.int32, so_ref.shape, 1)
    s_hot = (lane == target_column(s_targets, base)).astype(F32)
    t_hot = (lane == target_column(t_targets, base)).astype(F32)
    so_chance = jnp.exp(so_ref[...] - turned[:, 0:1])
    sm_chance = jnp.exp(sm_ref[...] - turned[:, 1:2])
    to_chance = jnp.exp(to_ref[...] - turned[:, 2:3])
    tm_chance = jnp.exp(tm_ref[...] - turned[:, 3:4])
    s_grad[...] = (live_column * (2.0 * so_chance - s_hot - sm_chance)).astype(BF16)
    t_grad[...] = (live_column * (2.0 * tm_chance - to_chance - t_hot)).astype(BF16)


def after(values, *needs):
    return lax.optimization_barrier((tuple(values), needs))[0]


def body(
    student_states,
    teacher_states,
    student_queries,
    teacher_keys,
    student_targets,
    teacher_targets,
    student_lengths,
    teacher_lengths,
    to_teacher,
    to_student,
    student_head,
    teacher_head,
):
    rows = student_states.shape[0]
    chips, sv_count = lax.axis_size("x"), lax.axis_size("sv")
    vocab = student_head.shape[1]
    tokens = rows // CORES
    sequences = teacher_lengths.shape[0]
    width = rows // sequences
    dma = pltpu.SemaphoreType.DMA

    def both(a):
        return lax.all_gather(a, "core", axis=0, tiled=True)

    def shift(a, axis, n):
        count = lax.axis_size(axis)
        return lax.ppermute(a, axis, [(i, (i + n) % count) for i in range(count)])

    def around(a, axis):
        return [shift(a, axis, n) for n in range(1, lax.axis_size(axis))]

    def cross(a, n):
        pairs = [(2 * i + c, (2 * (i + n) + 1 - c) % (CORES * chips)) for i in range(chips) for c in range(CORES)]
        return lax.ppermute(a, ("x", "core"), pairs)

    s_t, t_t = student_states.T, teacher_states.T
    w_t, w_s = to_teacher, to_student.T
    s_targets, t_targets = student_targets.reshape(1, rows), teacher_targets.reshape(1, rows)

    q_t, k_t = student_queries.T, teacher_keys.T
    qk = kernel_call(
        pack_kernel, shape((2 * q_t.shape[0], rows), BF16), [HBM] * 2, [dma((2,))], limit=60
    )(q_t, k_t)
    qk_blocks = [qk] + around(qk, "x") + [cross(qk, n) for n in range(chips)]
    chip_s, chip_w_t = (both(a) for a in after((s_t, w_t), qk))
    far_s, far_t = after((s_t, t_t), qk)
    far_s, far_t = around(far_s, "x"), around(far_t, "x")
    split = chips if w_t.shape[1] % (16 * chips) == 0 else 1
    share = shape((w_t.shape[1] // split, tokens))
    (chip_s, chip_w_t), qk_blocks = lax.optimization_barrier(((chip_s, chip_w_t), qk_blocks))
    *parts_t, _ = kernel_call(
        project, [share] * split + [shape((w_t.shape[1], tokens))], [VMEM] * 2
    )(chip_s, chip_w_t)

    t_out, w_out, *parts_t = lax.optimization_barrier((t_t, w_s, *parts_t))
    other_t = [shift(parts_t[n % split], "x", n) for n in range(1, chips)]
    chip_t, chip_w_s = both(t_out), both(w_out)
    features = q_t.shape[0] * chips * CORES
    part_s, weights = kernel_call(
        functools.partial(attend, len(qk_blocks)),
        (shape((w_s.shape[0], tokens)), shape((sequences, width, width), BF16)),
        [SMEM] + [VMEM] * (2 + len(qk_blocks)),
        [pltpu.VMEM((features, rows), BF16)] * 2,
    )(teacher_lengths, chip_t, chip_w_s, *qk_blocks)

    own_part, *other_t, part_s = lax.optimization_barrier((parts_t[0], *other_t, part_s))
    into_t = functools.reduce(jnp.add, other_t, own_part).astype(BF16)
    into_t = [into_t] + around(into_t, "sv")
    other_s = around(part_s, "x")

    far_s, far_t = [both(a) for a in far_s], [both(a) for a in far_t]

    *into_t, part_s = lax.optimization_barrier((*into_t, part_s))
    other_s = after(other_s, *into_t)
    into_s = functools.reduce(jnp.add, other_s, part_s).astype(BF16)
    into_s = [into_s] + around(into_s, "sv")
    into_t = kernel_call(
        functools.partial(collect, "sv"),
        shape((sv_count * into_t[0].shape[0], tokens), BF16),
        [VMEM] * sv_count,
    )(*into_t)
    t_shares = [into_t] + (around(into_t, "x") if split > 1 else [])
    t_shares = [both(a) for a in lax.optimization_barrier(tuple(t_shares))]
    s_blocks = [chip_s] + far_s
    t_blocks = [chip_t] + far_t
    logits = shape((rows, vocab))
    s_own, s_notes = kernel_call(
        own_student,
        (logits, shape((rows, 128))),
        [VMEM] * (2 + chips),
        [pltpu.VMEM((student_head.shape[0], rows), BF16)],
    )(s_targets, *s_blocks, student_head)
    t_own = kernel_call(
        own_teacher,
        logits,
        [VMEM] * (2 + chips),
        [pltpu.VMEM((teacher_head.shape[0], rows), BF16)],
    )(weights, *t_blocks, teacher_head)
    t_mapped, t_stats = kernel_call(
        mapped_teacher,
        (logits, shape((STATS, rows))),
        [VMEM] * (3 + len(t_shares)),
        [pltpu.VMEM((teacher_head.shape[0], rows), BF16)],
    )(t_targets, t_own, *t_shares, teacher_head)

    into_s = kernel_call(
        functools.partial(collect, "sv"),
        shape((sv_count * into_s[0].shape[0], tokens), BF16),
        [VMEM] * sv_count,
    )(*into_s)
    s_mapped, stats = kernel_call(
        student_side, (logits, shape((STATS, rows))), [VMEM] * 6
    )(s_targets, t_stats, s_own, s_notes, both(into_s), student_head)

    stats = lax.all_gather(stats, ("x", "core"), axis=0, tiled=True)
    stats = kernel_call(
        functools.partial(merge_kernel, chips * CORES), shape((STATS, rows)), [VMEM]
    )(stats)
    stats = [stats] + around(stats, "sv")
    s_loss, t_loss, s_grad, t_grad = kernel_call(
        functools.partial(finish, sv_count),
        (shape((1, rows)), shape((1, rows)), shape((rows, vocab), BF16), shape((rows, vocab), BF16)),
        [SMEM] + [VMEM] * (6 + sv_count),
    )(student_lengths, s_targets, t_targets, s_own, s_mapped, t_own, t_mapped, *stats)
    return s_loss.reshape(rows), t_loss.reshape(rows), s_grad, t_grad


def solution(mesh):
    grp, sv, tv = (mesh.shape[name] for name in ("grp", "sv", "tv"))
    devices = mesh.devices.reshape(grp, sv, tv // CORES, CORES)
    mesh = jax.sharding.Mesh(devices, ("grp", "sv", "x", "core"))
    tv = ("x", "core")
    columns = ("sv", "x", "core")
    in_specs = (P("grp", tv),) * 4 + (P("grp"),) * 4
    in_specs += (P(tv, "sv"),) * 2 + (P(None, columns),) * 2
    out_specs = (P("grp"), P("grp"), P("grp", columns), P("grp", columns))
    return jax.shard_map(body, mesh=mesh, in_specs=in_specs, out_specs=out_specs, check_vma=False)
```

```python
import functools

import jax
import jax.numpy as jnp
from jax import lax
from jax.experimental import pallas as pl
from jax.experimental.pallas import tpu as pltpu
from jax.sharding import PartitionSpec as P

DK = 256
FLOOR = -1e30
CORES = 2
STATS = 8
F32 = jnp.float32
BF16 = jnp.bfloat16

VMEM = pl.BlockSpec(memory_space=pltpu.VMEM)
SMEM = pl.BlockSpec(memory_space=pltpu.SMEM)
HBM = pl.BlockSpec(memory_space=pltpu.HBM)


def shape(dims, dtype=F32):
    return jax.ShapeDtypeStruct(dims, dtype)


def kernel_call(body, out_shape, in_specs, scratch=(), limit=32):
    single = not isinstance(out_shape, (tuple, list))
    return pl.pallas_call(
        body,
        out_shape=out_shape,
        in_specs=in_specs,
        out_specs=VMEM if single else [VMEM] * len(out_shape),
        scratch_shapes=list(scratch),
        compiler_params=pltpu.CompilerParams(vmem_limit_bytes=limit * 2**20),

    )


def dot00(a, b):
    return lax.dot_general(a, b, (((0,), (0,)), ((), ())), preferred_element_type=F32)


def dot10(a, b):
    return lax.dot_general(a, b, (((1,), (0,)), ((), ())), preferred_element_type=F32)


def part_of(index, width):
    return pl.ds(pl.multiple_of(index * width, width), width)


def behind(axis, offset):
    count = lax.axis_size(axis)
    return lax.rem(lax.axis_index(axis) - offset + count, count)


def block_place(n):
    core = lax.axis_index("core")
    return behind("x", n // CORES) * CORES + (core if n % CORES == 0 else 1 - core)


def vocab_base(vocab):
    place = lax.axis_index("sv") * lax.axis_size("x") + lax.axis_index("x")
    return (place * CORES + lax.axis_index("core")) * vocab


def fetch(sems, *pairs):
    copies = [pltpu.make_async_copy(a, b, sems.at[n]) for n, (a, b) in enumerate(pairs)]
    for copy in copies:
        copy.start()
    return copies


def pack_kernel(q_ref, k_ref, out_ref, sems):
    rows = q_ref.shape[0]
    for copy in fetch(sems, (q_ref, out_ref.at[:rows]), (k_ref, out_ref.at[rows:])):
        copy.wait()


def project(states, matrix, *out_refs):
    *shares, total = out_refs
    total[...] = dot00(matrix[...], states[:, part_of(lax.axis_index("core"), total.shape[1])])
    rows = shares[0].shape[0]
    for n, share in enumerate(shares):
        share[...] = total[part_of(behind("x", lax.axis_size("x") - n), rows), :]


def collect(axis, *refs):
    *blocks, out_ref = refs
    rows = blocks[0].shape[0]
    for n, block in enumerate(blocks):
        out_ref[part_of(behind(axis, n), rows), :] = block[...]


def attend(blocks, lens_ref, own_t, own_w, mate_t, mate_w, *refs):
    qk_refs = refs[:blocks]
    out_ref, weights_ref, q_all, k_all, t_v, w_v, sems = refs[blocks:]
    copies = fetch(sems, (own_t, t_v), (own_w, w_v))
    rows = qk_refs[0].shape[0] // 2
    for n, ref in enumerate(qk_refs):
        q_all[n * rows : (n + 1) * rows, :] = ref[:rows]
        k_all[n * rows : (n + 1) * rows, :] = ref[rows:]
    sequences = lens_ref.shape[0]
    width = q_all.shape[1] // sequences
    for s in range(sequences):
        tokens = slice(s * width, (s + 1) * width)
        scores = dot00(k_all[:, tokens], q_all[:, tokens]) * DK ** (-0.5)
        position = lax.broadcasted_iota(jnp.int32, scores.shape, 0)
        scores = jnp.where(position < lens_ref[s], scores, FLOOR)
        raised = jnp.exp(scores - jnp.max(scores, axis=0, keepdims=True))
        weights_ref[s] = (raised / jnp.sum(raised, axis=0, keepdims=True)).astype(BF16)
    for copy in copies:
        copy.wait()
    per_core = sequences // CORES
    for n in range(per_core):
        s = lax.axis_index("core") * per_core + n
        tokens = part_of(s, width)
        own = dot10(t_v[:, tokens], weights_ref[s]).astype(BF16)
        mate = dot10(mate_t[:, tokens], weights_ref[s]).astype(BF16)
        out_ref[:, n * width : (n + 1) * width] = dot10(w_v[...], own) + dot10(mate_w[...], mate)


def log_total(logits):
    highest = jnp.max(logits, axis=1, keepdims=True)
    raised = jnp.exp(logits - highest)
    summed = jnp.sum(raised, axis=1, keepdims=True)
    return raised, summed, highest + jnp.log(summed)


def target_column(ref, base):
    row = jnp.broadcast_to((ref[...] - base).astype(F32), (STATS, ref.shape[1]))
    return jnp.transpose(row)[:, 0:1].astype(jnp.int32)


def pick(logits, columns):
    lane = lax.broadcasted_iota(jnp.int32, logits.shape, 1)
    return jnp.sum(jnp.where(lane == columns, logits, 0.0), axis=1, keepdims=True)


def pack_columns(columns):
    lane = lax.broadcasted_iota(jnp.int32, (columns[0].shape[0], 128), 1)
    packed = jnp.zeros(lane.shape, F32)
    for k, column in enumerate(columns):
        packed = jnp.where(lane == k, column, packed)
    return packed


def own_student(targets, *refs):
    chip, *blocks, head, out_ref, notes_ref, s_all = refs
    s_all[part_of(lax.axis_index("x"), chip.shape[0]), :] = chip[...]
    for n, block in enumerate(blocks):
        s_all[part_of(block_place(n + CORES), block.shape[0]), :] = block[...]
    logits = dot00(s_all[...], head[...])
    out_ref[...] = logits
    columns = target_column(targets, vocab_base(head.shape[1]))
    _, _, total = log_total(logits)
    notes_ref[...] = pack_columns((total, pick(logits, columns)))


def own_teacher(weights_ref, own_t, *refs):
    *blocks, head, own_ref, t_v, t_all, sems = refs
    copies = fetch(sems, (own_t, t_v))
    sequences, width, _ = weights_ref.shape
    rows = own_t.shape[0]
    for copy in copies:
        copy.wait()
    for n, block in enumerate([t_v] + blocks):
        for s in range(sequences):
            tokens = slice(s * width, (s + 1) * width)
            aligned = dot10(block[:, tokens], weights_ref[s]).astype(BF16)
            t_all[part_of(block_place(n), rows), tokens] = aligned
    own_ref[...] = dot00(t_all[...], head[...])


def mapped_teacher(targets, own_ref, *refs):
    *shares, head, mapped_ref, stats_ref, t_all = refs
    parts, blocks = len(shares), lax.axis_size("sv")
    width = shares[0].shape[1]
    rows = shares[0].shape[0] // (CORES * blocks)
    for n, share in enumerate(shares):
        part = behind("x", n) if parts > 1 else 0
        for c in range(CORES):
            tokens = slice(c * width, (c + 1) * width)
            for z in range(blocks):
                place = (c * blocks + z) * rows
                t_all[part_of(z * parts + part, rows), tokens] = share[place : place + rows, :]
    mapped = dot00(t_all[...], head[...])
    mapped_ref[...] = mapped
    own = own_ref[...]
    columns = target_column(targets, vocab_base(head.shape[1]))
    raised, summed, own_total = log_total(own)
    _, _, mapped_total = log_total(mapped)
    spread = jnp.sum(raised * (own - mapped), axis=1, keepdims=True) / summed
    zero = jnp.zeros_like(spread)
    columns = (zero, zero, own_total, mapped_total, zero, zero, spread, pick(mapped, columns))
    stats_ref[...] = jnp.transpose(pack_columns(columns))[:STATS]


def student_side(targets, t_stats, own_ref, notes_ref, halves, head, mapped_ref, stats_ref):
    rows = halves.shape[0] // CORES
    states = jnp.concatenate([halves[:rows], halves[rows:]], axis=1)
    mapped = dot00(states, head[...])
    mapped_ref[...] = mapped
    columns = target_column(targets, vocab_base(head.shape[1]))
    raised, summed, total = log_total(mapped)
    spread = jnp.sum(raised * (mapped - own_ref[...]), axis=1, keepdims=True) / summed
    zero = jnp.zeros_like(spread)
    picked = notes_ref[:, 1:2] + pick(mapped, columns)
    columns = (notes_ref[:, 0:1], total, zero, zero, spread, picked)
    stats_ref[...] = jnp.transpose(pack_columns(columns))[:STATS] + t_stats[...]


def merge_stats(parts):
    highest = parts[0]
    for part in parts[1:]:
        highest = jnp.maximum(highest, part)
    total = highest + jnp.log(sum(jnp.exp(part - highest) for part in parts))
    shares = [jnp.exp(part - total) for part in parts]
    s_spread = sum(share[1:2] * part[4:5] for share, part in zip(shares, parts))
    s_picked = sum(part[5:6] for part in parts)
    t_spread = sum(share[2:3] * part[6:7] for share, part in zip(shares, parts))
    t_picked = sum(part[7:8] for part in parts)
    return total, s_spread, s_picked, t_spread, t_picked


def merge_kernel(parts, in_ref, out_ref):
    total, *rest = merge_stats([in_ref[n * STATS : (n + 1) * STATS, :] for n in range(parts)])
    row = lax.broadcasted_iota(jnp.int32, total.shape, 0)
    for k, value in enumerate(rest):
        total = jnp.where(row == 4 + k, value, total)
    out_ref[...] = total


def finish(parts, lens_ref, s_targets, t_targets, so_ref, sm_ref, to_ref, tm_ref, *refs):
    s_loss, t_loss, s_grad, t_grad = refs[parts:]
    totals, s_spread, s_picked, t_spread, t_picked = merge_stats([ref[...] for ref in refs[:parts]])
    so, sm, to, tm = (totals[k : k + 1] for k in range(4))
    rows = s_loss.shape[1]
    sequences = lens_ref.shape[0]
    width = rows // sequences

    def live(dims, dim):
        place = lax.broadcasted_iota(jnp.int32, dims, dim)
        mask = jnp.zeros(dims, jnp.bool_)
        for s in range(sequences):
            mask |= (place >= s * width) & (place < s * width + lens_ref[s])
        return mask.astype(F32)

    live_row = live((1, rows), 1)
    s_loss[...] = live_row * (so + sm - s_picked + (s_spread - sm + so))
    t_loss[...] = live_row * ((t_spread - to + tm) + tm - t_picked)
    turned = jnp.transpose(totals)
    live_column = live((rows, 1), 0)
    base = vocab_base(so_ref.shape[1])
    lane = lax.broadcasted_iota(jnp.int32, so_ref.shape, 1)
    s_hot = (lane == target_column(s_targets, base)).astype(F32)
    t_hot = (lane == target_column(t_targets, base)).astype(F32)
    so_chance = jnp.exp(so_ref[...] - turned[:, 0:1])
    sm_chance = jnp.exp(sm_ref[...] - turned[:, 1:2])
    to_chance = jnp.exp(to_ref[...] - turned[:, 2:3])
    tm_chance = jnp.exp(tm_ref[...] - turned[:, 3:4])
    s_grad[...] = (live_column * (2.0 * so_chance - s_hot - sm_chance)).astype(BF16)
    t_grad[...] = (live_column * (2.0 * tm_chance - to_chance - t_hot)).astype(BF16)


def after(values, *needs):
    return lax.optimization_barrier((tuple(values), needs))[0]


def body(
    student_states,
    teacher_states,
    student_queries,
    teacher_keys,
    student_targets,
    teacher_targets,
    student_lengths,
    teacher_lengths,
    to_teacher,
    to_student,
    student_head,
    teacher_head,
):
    rows = student_states.shape[0]
    chips, sv_count = lax.axis_size("x"), lax.axis_size("sv")
    vocab = student_head.shape[1]
    tokens = rows // CORES
    sequences = teacher_lengths.shape[0]
    width = rows // sequences
    dma = pltpu.SemaphoreType.DMA

    def both(a):
        return lax.all_gather(a, "core", axis=0, tiled=True)

    def swap(a):
        return lax.ppermute(a, "core", [(0, 1), (1, 0)])

    def shift(a, axis, n):
        count = lax.axis_size(axis)
        return lax.ppermute(a, axis, [(i, (i + n) % count) for i in range(count)])

    def around(a, axis):
        return [shift(a, axis, n) for n in range(1, lax.axis_size(axis))]

    def cross(a, n):
        pairs = [(2 * i + c, (2 * (i + n) + 1 - c) % (CORES * chips)) for i in range(chips) for c in range(CORES)]
        return lax.ppermute(a, ("x", "core"), pairs)

    s_t, t_t = student_states.T, teacher_states.T
    w_t, w_s = to_teacher, to_student.T
    s_targets, t_targets = student_targets.reshape(1, rows), teacher_targets.reshape(1, rows)

    q_t, k_t = student_queries.T, teacher_keys.T
    qk = kernel_call(
        pack_kernel, shape((2 * q_t.shape[0], rows), BF16), [HBM] * 2, [dma((2,))], limit=60
    )(q_t, k_t)
    qk_blocks = [qk] + around(qk, "x") + [cross(qk, n) for n in range(chips)]
    mate_w_s, mate_t = swap(w_s), swap(t_t)
    chip_w_t, chip_s = (both(a) for a in after((w_t, s_t), qk))
    far_s = around(after((s_t,), qk)[0], "x")
    split = chips if w_t.shape[1] % (16 * chips) == 0 else 1
    share = shape((w_t.shape[1] // split, tokens))
    *parts_t, _ = kernel_call(
        project, [share] * split + [shape((w_t.shape[1], tokens))], [VMEM] * 2
    )(chip_s, chip_w_t)

    *qk_blocks, mate_w_s, mate_t, parts_t = lax.optimization_barrier(
        (*qk_blocks, mate_w_s, mate_t, parts_t)
    )
    other_t = [shift(parts_t[n % split], "x", n) for n in range(1, chips)]
    features = q_t.shape[0] * chips * CORES
    part_s, weights = kernel_call(
        functools.partial(attend, len(qk_blocks)),
        (shape((w_s.shape[0], tokens)), shape((sequences, width, width), BF16)),
        [SMEM] + [HBM] * 2 + [VMEM] * (2 + len(qk_blocks)),
        [pltpu.VMEM((features, rows), BF16)] * 2
        + [pltpu.VMEM(a.shape, BF16) for a in (t_t, w_s)]
        + [dma((2,))],
    )(teacher_lengths, t_t, w_s, mate_t, mate_w_s, *qk_blocks)

    own_part, *other_t, part_s = lax.optimization_barrier((parts_t[0], *other_t, part_s))
    far_t = around(after((t_t,), *other_t)[0], "x")
    into_t = functools.reduce(jnp.add, other_t, own_part).astype(BF16)
    into_t = [into_t] + around(into_t, "sv")
    other_s = around(part_s, "x")

    *into_t, part_s, other_s = lax.optimization_barrier((*into_t, part_s, other_s))
    into_s = functools.reduce(jnp.add, other_s, part_s).astype(BF16)
    into_s = [into_s] + around(into_s, "sv")
    into_t = kernel_call(
        functools.partial(collect, "sv"),
        shape((sv_count * into_t[0].shape[0], tokens), BF16),
        [VMEM] * sv_count,
    )(*into_t)
    t_shares = [into_t] + (around(into_t, "x") if split > 1 else [])
    t_shares = [both(a) for a in t_shares]
    s_blocks = [chip_s] + [p for a in far_s for p in (a, swap(a))]
    t_blocks = [mate_t] + [p for a in far_t for p in (a, swap(a))]
    logits = shape((rows, vocab))
    s_own, s_notes = kernel_call(
        own_student,
        (logits, shape((rows, 128))),
        [VMEM] * (2 + len(s_blocks)),
        [pltpu.VMEM((student_head.shape[0], rows), BF16)],
    )(s_targets, *s_blocks, student_head)
    t_own = kernel_call(
        own_teacher,
        logits,
        [VMEM, HBM] + [VMEM] * (1 + len(t_blocks)),
        [
            pltpu.VMEM(t_t.shape, BF16),
            pltpu.VMEM((teacher_head.shape[0], rows), BF16),
            dma((1,)),
        ],
    )(weights, t_t, *t_blocks, teacher_head)
    t_mapped, t_stats = kernel_call(
        mapped_teacher,
        (logits, shape((STATS, rows))),
        [VMEM] * (3 + len(t_shares)),
        [pltpu.VMEM((teacher_head.shape[0], rows), BF16)],
    )(t_targets, t_own, *t_shares, teacher_head)

    into_s = kernel_call(
        functools.partial(collect, "sv"),
        shape((sv_count * into_s[0].shape[0], tokens), BF16),
        [VMEM] * sv_count,
    )(*after(into_s, t_stats))
    s_mapped, stats = kernel_call(
        student_side, (logits, shape((STATS, rows))), [VMEM] * 6
    )(s_targets, t_stats, s_own, s_notes, both(into_s), student_head)

    stats = lax.all_gather(stats, ("x", "core"), axis=0, tiled=True)
    stats = kernel_call(
        functools.partial(merge_kernel, chips * CORES), shape((STATS, rows)), [VMEM]
    )(stats)
    stats = [stats] + around(stats, "sv")
    s_loss, t_loss, s_grad, t_grad = kernel_call(
        functools.partial(finish, sv_count),
        (shape((1, rows)), shape((1, rows)), shape((rows, vocab), BF16), shape((rows, vocab), BF16)),
        [SMEM] + [VMEM] * (6 + sv_count),
    )(student_lengths, s_targets, t_targets, s_own, s_mapped, t_own, t_mapped, *stats)
    return s_loss.reshape(rows), t_loss.reshape(rows), s_grad, t_grad


def solution(mesh):
    grp, sv, tv = (mesh.shape[name] for name in ("grp", "sv", "tv"))
    devices = mesh.devices.reshape(grp, sv, tv // CORES, CORES)
    mesh = jax.sharding.Mesh(devices, ("grp", "sv", "x", "core"))
    tv = ("x", "core")
    columns = ("sv", "x", "core")
    in_specs = (P("grp", tv),) * 4 + (P("grp"),) * 4
    in_specs += (P(tv, "sv"),) * 2 + (P(None, columns),) * 2
    out_specs = (P("grp"), P("grp"), P("grp", columns), P("grp", columns))
    return jax.shard_map(body, mesh=mesh, in_specs=in_specs, out_specs=out_specs, check_vma=False)
```

```python
import functools

import jax
import jax.numpy as jnp
from jax import lax
from jax.experimental import pallas as pl
from jax.experimental.pallas import tpu as pltpu
from jax.sharding import PartitionSpec as P

DK = 256
FLOOR = -1e30
CORES = 2
STATS = 8
F32 = jnp.float32
BF16 = jnp.bfloat16

VMEM = pl.BlockSpec(memory_space=pltpu.VMEM)
SMEM = pl.BlockSpec(memory_space=pltpu.SMEM)
HBM = pl.BlockSpec(memory_space=pltpu.HBM)


def shape(dims, dtype=F32):
    return jax.ShapeDtypeStruct(dims, dtype)


def kernel_call(body, out_shape, in_specs, scratch=(), limit=32):
    single = not isinstance(out_shape, (tuple, list))
    return pl.pallas_call(
        body,
        out_shape=out_shape,
        in_specs=in_specs,
        out_specs=VMEM if single else [VMEM] * len(out_shape),
        scratch_shapes=list(scratch),
        compiler_params=pltpu.CompilerParams(vmem_limit_bytes=limit * 2**20),

    )


def dot00(a, b):
    return lax.dot_general(a, b, (((0,), (0,)), ((), ())), preferred_element_type=F32)


def dot10(a, b):
    return lax.dot_general(a, b, (((1,), (0,)), ((), ())), preferred_element_type=F32)


def part_of(index, width):
    return pl.ds(pl.multiple_of(index * width, width), width)


def behind(axis, offset):
    count = lax.axis_size(axis)
    return lax.rem(lax.axis_index(axis) - offset + count, count)


def block_place(n):
    core = lax.axis_index("core")
    return behind("x", n // CORES) * CORES + (core if n % CORES == 0 else 1 - core)


def vocab_base(vocab):
    place = lax.axis_index("sv") * lax.axis_size("x") + lax.axis_index("x")
    return (place * CORES + lax.axis_index("core")) * vocab


def fetch(sems, *pairs):
    copies = [pltpu.make_async_copy(a, b, sems.at[n]) for n, (a, b) in enumerate(pairs)]
    for copy in copies:
        copy.start()
    return copies


def prepare(q_ref, k_ref, own_s, own_w, qk_ref, keep_ref, give_ref, s_v, w_v, sems):
    rows = q_ref.shape[0]
    qk_pairs = (q_ref, qk_ref.at[:rows]), (k_ref, qk_ref.at[rows:])
    copies = fetch(sems, (own_s, s_v), (own_w, w_v), *qk_pairs)
    for copy in copies:
        copy.wait()
    core = lax.axis_index("core")
    tokens = keep_ref.shape[1]
    give_ref[...] = dot00(w_v[...], s_v[:, part_of(1 - core, tokens)])
    keep_ref[...] = dot00(w_v[...], s_v[:, part_of(core, tokens)])


def share_out(keep_ref, got_ref, *shares):
    rows = shares[0].shape[0]
    for n, share in enumerate(shares):
        place = part_of(behind("x", lax.axis_size("x") - n), rows) if len(shares) > 1 else slice(None)
        share[...] = keep_ref[place, :] + got_ref[place, :]


def collect(axis, *refs):
    *blocks, out_ref = refs
    rows = blocks[0].shape[0]
    for n, block in enumerate(blocks):
        out_ref[part_of(behind(axis, n), rows), :] = block[...]


def attend(blocks, lens_ref, states, matrix, *refs):
    qk_refs = refs[:blocks]
    out_ref, weights_ref, q_all, k_all = refs[blocks:]
    rows = qk_refs[0].shape[0] // 2
    for n, ref in enumerate(qk_refs):
        q_all[n * rows : (n + 1) * rows, :] = ref[:rows]
        k_all[n * rows : (n + 1) * rows, :] = ref[rows:]
    sequences = lens_ref.shape[0]
    width = q_all.shape[1] // sequences
    for s in range(sequences):
        tokens = slice(s * width, (s + 1) * width)
        scores = dot00(k_all[:, tokens], q_all[:, tokens]) * DK ** (-0.5)
        position = lax.broadcasted_iota(jnp.int32, scores.shape, 0)
        scores = jnp.where(position < lens_ref[s], scores, FLOOR)
        raised = jnp.exp(scores - jnp.max(scores, axis=0, keepdims=True))
        weights_ref[s] = (raised / jnp.sum(raised, axis=0, keepdims=True)).astype(BF16)
    per_core = sequences // CORES
    rows, cols = states.shape[0] // CORES, out_ref.shape[0]
    for n in range(per_core):
        s = lax.axis_index("core") * per_core + n
        aligned = dot10(states[:, part_of(s, width)], weights_ref[s]).astype(BF16)
        total = sum(
            dot10(matrix[c * cols : (c + 1) * cols, :], aligned[c * rows : (c + 1) * rows])
            for c in range(CORES)
        )
        out_ref[:, n * width : (n + 1) * width] = total


def log_total(logits):
    highest = jnp.max(logits, axis=1, keepdims=True)
    raised = jnp.exp(logits - highest)
    summed = jnp.sum(raised, axis=1, keepdims=True)
    return raised, summed, highest + jnp.log(summed)


def target_column(ref, base):
    row = jnp.broadcast_to((ref[...] - base).astype(F32), (STATS, ref.shape[1]))
    return jnp.transpose(row)[:, 0:1].astype(jnp.int32)


def pick(logits, columns):
    lane = lax.broadcasted_iota(jnp.int32, logits.shape, 1)
    return jnp.sum(jnp.where(lane == columns, logits, 0.0), axis=1, keepdims=True)


def pack_columns(columns):
    lane = lax.broadcasted_iota(jnp.int32, (columns[0].shape[0], 128), 1)
    packed = jnp.zeros(lane.shape, F32)
    for k, column in enumerate(columns):
        packed = jnp.where(lane == k, column, packed)
    return packed


def own_student(targets, own_s, mate_s, *refs):
    *chips, head, out_ref, notes_ref, s_all, sems = refs
    rows = own_s.shape[0]
    copies = fetch(sems, (own_s, s_all.at[part_of(block_place(0), rows), :]))
    s_all[part_of(block_place(1), rows), :] = mate_s[...]
    for n, chip in enumerate(chips):
        s_all[part_of(behind("x", n + 1), CORES * rows), :] = chip[...]
    for copy in copies:
        copy.wait()
    logits = dot00(s_all[...], head[...])
    out_ref[...] = logits
    columns = target_column(targets, vocab_base(head.shape[1]))
    _, _, total = log_total(logits)
    notes_ref[...] = pack_columns((total, pick(logits, columns)))


def own_teacher(weights_ref, *refs):
    *chips, head, own_ref, t_all = refs
    sequences, width, _ = weights_ref.shape
    rows = chips[0].shape[0]
    for n, chip in enumerate(chips):
        for s in range(sequences):
            tokens = slice(s * width, (s + 1) * width)
            aligned = dot10(chip[:, tokens], weights_ref[s]).astype(BF16)
            t_all[part_of(behind("x", n), rows), tokens] = aligned
    own_ref[...] = dot00(t_all[...], head[...])


def mapped_teacher(targets, own_ref, *refs):
    *shares, head, mapped_ref, stats_ref, t_all = refs
    parts, blocks = len(shares), lax.axis_size("sv")
    width = shares[0].shape[1]
    rows = shares[0].shape[0] // (CORES * blocks)
    for n, share in enumerate(shares):
        part = behind("x", n) if parts > 1 else 0
        for c in range(CORES):
            tokens = slice(c * width, (c + 1) * width)
            for z in range(blocks):
                place = (c * blocks + z) * rows
                t_all[part_of(z * parts + part, rows), tokens] = share[place : place + rows, :]
    mapped = dot00(t_all[...], head[...])
    mapped_ref[...] = mapped
    own = own_ref[...]
    columns = target_column(targets, vocab_base(head.shape[1]))
    raised, summed, own_total = log_total(own)
    _, _, mapped_total = log_total(mapped)
    spread = jnp.sum(raised * (own - mapped), axis=1, keepdims=True) / summed
    zero = jnp.zeros_like(spread)
    columns = (zero, zero, own_total, mapped_total, zero, zero, spread, pick(mapped, columns))
    stats_ref[...] = jnp.transpose(pack_columns(columns))[:STATS]


def student_side(targets, t_stats, own_ref, notes_ref, halves, head, mapped_ref, stats_ref):
    rows = halves.shape[0] // CORES
    states = jnp.concatenate([halves[:rows], halves[rows:]], axis=1)
    mapped = dot00(states, head[...])
    mapped_ref[...] = mapped
    columns = target_column(targets, vocab_base(head.shape[1]))
    raised, summed, total = log_total(mapped)
    spread = jnp.sum(raised * (mapped - own_ref[...]), axis=1, keepdims=True) / summed
    zero = jnp.zeros_like(spread)
    picked = notes_ref[:, 1:2] + pick(mapped, columns)
    columns = (notes_ref[:, 0:1], total, zero, zero, spread, picked)
    stats_ref[...] = jnp.transpose(pack_columns(columns))[:STATS] + t_stats[...]


def merge_stats(parts):
    highest = parts[0]
    for part in parts[1:]:
        highest = jnp.maximum(highest, part)
    total = highest + jnp.log(sum(jnp.exp(part - highest) for part in parts))
    shares = [jnp.exp(part - total) for part in parts]
    s_spread = sum(share[1:2] * part[4:5] for share, part in zip(shares, parts))
    s_picked = sum(part[5:6] for part in parts)
    t_spread = sum(share[2:3] * part[6:7] for share, part in zip(shares, parts))
    t_picked = sum(part[7:8] for part in parts)
    return total, s_spread, s_picked, t_spread, t_picked


def merge_kernel(*refs):
    *parts, out_ref = refs
    total, *rest = merge_stats([part[...] for part in parts])
    row = lax.broadcasted_iota(jnp.int32, total.shape, 0)
    for k, value in enumerate(rest):
        total = jnp.where(row == 4 + k, value, total)
    out_ref[...] = total


def finish(parts, lens_ref, s_targets, t_targets, so_ref, sm_ref, to_ref, tm_ref, *refs):
    s_loss, t_loss, s_grad, t_grad = refs[parts:]
    totals, s_spread, s_picked, t_spread, t_picked = merge_stats([ref[...] for ref in refs[:parts]])
    so, sm, to, tm = (totals[k : k + 1] for k in range(4))
    rows = s_loss.shape[1]
    sequences = lens_ref.shape[0]
    width = rows // sequences

    def live(dims, dim):
        place = lax.broadcasted_iota(jnp.int32, dims, dim)
        mask = jnp.zeros(dims, jnp.bool_)
        for s in range(sequences):
            mask |= (place >= s * width) & (place < s * width + lens_ref[s])
        return mask.astype(F32)

    live_row = live((1, rows), 1)
    s_loss[...] = live_row * (so + sm - s_picked + (s_spread - sm + so))
    t_loss[...] = live_row * ((t_spread - to + tm) + tm - t_picked)
    turned = jnp.transpose(totals)
    live_column = live((rows, 1), 0)
    base = vocab_base(so_ref.shape[1])
    lane = lax.broadcasted_iota(jnp.int32, so_ref.shape, 1)
    s_hot = (lane == target_column(s_targets, base)).astype(F32)
    t_hot = (lane == target_column(t_targets, base)).astype(F32)
    so_chance = jnp.exp(so_ref[...] - turned[:, 0:1])
    sm_chance = jnp.exp(sm_ref[...] - turned[:, 1:2])
    to_chance = jnp.exp(to_ref[...] - turned[:, 2:3])
    tm_chance = jnp.exp(tm_ref[...] - turned[:, 3:4])
    s_grad[...] = (live_column * (2.0 * so_chance - s_hot - sm_chance)).astype(BF16)
    t_grad[...] = (live_column * (2.0 * tm_chance - to_chance - t_hot)).astype(BF16)


def after(values, *needs):
    return lax.optimization_barrier((tuple(values), needs))[0]


def body(
    student_states,
    teacher_states,
    student_queries,
    teacher_keys,
    student_targets,
    teacher_targets,
    student_lengths,
    teacher_lengths,
    to_teacher,
    to_student,
    student_head,
    teacher_head,
):
    rows = student_states.shape[0]
    chips, sv_count = lax.axis_size("x"), lax.axis_size("sv")
    vocab = student_head.shape[1]
    tokens = rows // CORES
    sequences = teacher_lengths.shape[0]
    width = rows // sequences
    dma = pltpu.SemaphoreType.DMA

    def both(a):
        return lax.all_gather(a, "core", axis=0, tiled=True)

    def swap(a):
        return lax.ppermute(a, "core", [(0, 1), (1, 0)])

    def shift(a, axis, n):
        count = lax.axis_size(axis)
        return lax.ppermute(a, axis, [(i, (i + n) % count) for i in range(count)])

    def around(a, axis):
        return [shift(a, axis, n) for n in range(1, lax.axis_size(axis))]

    def cross(a, n):
        pairs = [(2 * i + c, (2 * (i + n) + 1 - c) % (CORES * chips)) for i in range(chips) for c in range(CORES)]
        return lax.ppermute(a, ("x", "core"), pairs)

    s_t, t_t = student_states.T, teacher_states.T
    w_t, w_s = to_teacher, to_student.T
    s_targets, t_targets = student_targets.reshape(1, rows), teacher_targets.reshape(1, rows)

    qk, keep, give = kernel_call(
        prepare,
        [shape((2 * student_queries.shape[1], rows), BF16)] + [shape((w_t.shape[1], tokens))] * 2,
        [HBM] * 4,
        [pltpu.VMEM(a.shape, BF16) for a in (s_t, w_t)] + [dma((4,))],
        limit=60,
    )(student_queries.T, teacher_keys.T, s_t, w_t)
    got = swap(give)
    qk_blocks = [qk] + around(qk, "x") + [cross(qk, n) for n in range(chips)]
    split = chips if w_t.shape[1] % (16 * chips) == 0 else 1
    parts_t = kernel_call(
        share_out, [shape((w_t.shape[1] // split, tokens))] * split, [VMEM] * 2
    )(keep, got)

    s_out, t_out, w_out, *parts_t = lax.optimization_barrier((s_t, t_t, w_s, *parts_t))
    other_t = [shift(parts_t[n % split], "x", n) for n in range(1, chips)]
    chip_w_s, chip_t = both(w_out), both(t_out)
    mate_s = swap(s_out)
    far_s = around(after((s_t,), chip_t, chip_w_s)[0], "x")
    features = student_queries.shape[1] * chips * CORES
    part_s, weights = kernel_call(
        functools.partial(attend, len(qk_blocks)),
        (shape((w_s.shape[0], tokens)), shape((sequences, width, width), BF16)),
        [SMEM] + [VMEM] * (2 + len(qk_blocks)),
        [pltpu.VMEM((features, rows), BF16)] * 2,
    )(teacher_lengths, chip_t, chip_w_s, *qk_blocks)

    own_part, *other_t, part_s, mate_s = lax.optimization_barrier(
        (parts_t[0], *other_t, part_s, mate_s)
    )
    into_t = functools.reduce(jnp.add, other_t, own_part).astype(BF16)
    into_t = [into_t] + around(into_t, "sv")
    other_s = around(part_s, "x")
    far_t = around(after((t_t,), *other_t)[0], "x")
    s_blocks = [both(a) for a in after(far_s, *other_t)]

    logits = shape((rows, vocab))
    s_own, s_notes = kernel_call(
        own_student,
        (logits, shape((rows, 128))),
        [VMEM, HBM] + [VMEM] * (2 + len(s_blocks)),
        [pltpu.VMEM((student_head.shape[0], rows), BF16), dma((1,))],
    )(s_targets, s_t, mate_s, *s_blocks, student_head)

    *into_t, part_s, other_s, s_own = lax.optimization_barrier((*into_t, part_s, other_s, s_own))
    into_t = kernel_call(
        functools.partial(collect, "sv"),
        shape((sv_count * into_t[0].shape[0], tokens), BF16),
        [VMEM] * sv_count,
    )(*into_t)
    into_t, part_s = lax.optimization_barrier((into_t, part_s))
    into_s = functools.reduce(jnp.add, other_s, part_s).astype(BF16)
    into_s = [into_s] + around(into_s, "sv")
    t_shares = [into_t] + (around(into_t, "x") if split > 1 else [])
    t_shares = [both(a) for a in t_shares]
    t_blocks = [chip_t] + [both(a) for a in far_t]
    t_own = kernel_call(
        own_teacher,
        logits,
        [VMEM] * (2 + len(t_blocks)),
        [pltpu.VMEM((teacher_head.shape[0], rows), BF16)],
    )(weights, *t_blocks, teacher_head)
    t_mapped, t_stats = kernel_call(
        mapped_teacher,
        (logits, shape((STATS, rows))),
        [VMEM] * (3 + len(t_shares)),
        [pltpu.VMEM((teacher_head.shape[0], rows), BF16)],
    )(t_targets, t_own, *t_shares, teacher_head)

    into_s = kernel_call(
        functools.partial(collect, "sv"),
        shape((sv_count * into_s[0].shape[0], tokens), BF16),
        [VMEM] * sv_count,
    )(*after(into_s, t_stats))
    s_mapped, stats = kernel_call(
        student_side, (logits, shape((STATS, rows))), [VMEM] * 6
    )(s_targets, t_stats, s_own, s_notes, both(into_s), student_head)

    stats = [stats] + around(stats, "x") + [cross(stats, n) for n in range(chips)]
    stats = kernel_call(merge_kernel, shape((STATS, rows)), [VMEM] * len(stats))(*stats)
    stats = [stats] + around(stats, "sv")
    s_loss, t_loss, s_grad, t_grad = kernel_call(
        functools.partial(finish, sv_count),
        (shape((1, rows)), shape((1, rows)), shape((rows, vocab), BF16), shape((rows, vocab), BF16)),
        [SMEM] + [VMEM] * (6 + sv_count),
    )(student_lengths, s_targets, t_targets, s_own, s_mapped, t_own, t_mapped, *stats)
    return s_loss.reshape(rows), t_loss.reshape(rows), s_grad, t_grad


def solution(mesh):
    grp, sv, tv = (mesh.shape[name] for name in ("grp", "sv", "tv"))
    devices = mesh.devices.reshape(grp, sv, tv // CORES, CORES)
    mesh = jax.sharding.Mesh(devices, ("grp", "sv", "x", "core"))
    tv = ("x", "core")
    columns = ("sv", "x", "core")
    in_specs = (P("grp", tv),) * 4 + (P("grp"),) * 4
    in_specs += (P(tv, "sv"),) * 2 + (P(None, columns),) * 2
    out_specs = (P("grp"), P("grp"), P("grp", columns), P("grp", columns))
    return jax.shard_map(body, mesh=mesh, in_specs=in_specs, out_specs=out_specs, check_vma=False)
```

```python
import functools

import jax
import jax.numpy as jnp
from jax import lax
from jax.experimental import pallas as pl
from jax.experimental.pallas import tpu as pltpu
from jax.sharding import PartitionSpec as P

DK = 256
FLOOR = -1e30
CORES = 2
STATS = 8
F32 = jnp.float32
BF16 = jnp.bfloat16

VMEM = pl.BlockSpec(memory_space=pltpu.VMEM)
SMEM = pl.BlockSpec(memory_space=pltpu.SMEM)
HBM = pl.BlockSpec(memory_space=pltpu.HBM)


def shape(dims, dtype=F32):
    return jax.ShapeDtypeStruct(dims, dtype)


def kernel_call(body, out_shape, in_specs, scratch=(), limit=32, outs=VMEM):
    single = not isinstance(out_shape, (tuple, list))
    return pl.pallas_call(
        body,
        out_shape=out_shape,
        in_specs=in_specs,
        out_specs=outs if single else [outs] * len(out_shape),
        scratch_shapes=list(scratch),
        compiler_params=pltpu.CompilerParams(vmem_limit_bytes=limit * 2**20),

    )


def dot00(a, b):
    return lax.dot_general(a, b, (((0,), (0,)), ((), ())), preferred_element_type=F32)


def dot10(a, b):
    return lax.dot_general(a, b, (((1,), (0,)), ((), ())), preferred_element_type=F32)


def part_of(index, width):
    return pl.ds(pl.multiple_of(index * width, width), width)


def behind(axis, offset):
    count = lax.axis_size(axis)
    return lax.rem(lax.axis_index(axis) - offset + count, count)


def block_place(n):
    core = lax.axis_index("core")
    return behind("x", n // CORES) * CORES + (core if n % CORES == 0 else 1 - core)


def vocab_base(vocab):
    place = lax.axis_index("sv") * lax.axis_size("x") + lax.axis_index("x")
    return (place * CORES + lax.axis_index("core")) * vocab


def fetch(sems, *pairs):
    copies = [pltpu.make_async_copy(a, b, sems.at[n]) for n, (a, b) in enumerate(pairs)]
    for copy in copies:
        copy.start()
    return copies


def prepare(q_ref, k_ref, own_s, own_w, qk_ref, keep_ref, give_ref, s_v, w_v, total, sems):
    rows = q_ref.shape[0]
    qk_pairs = (q_ref, qk_ref.at[:rows]), (k_ref, qk_ref.at[rows:])
    copies = fetch(sems, (own_s, s_v), (own_w, w_v), *qk_pairs)
    for copy in copies:
        copy.wait()
    core = lax.axis_index("core")
    tokens = keep_ref.shape[1]
    total[...] = dot00(w_v[...], s_v[...])
    give_ref[...] = total[:, part_of(1 - core, tokens)]
    keep_ref[...] = total[:, part_of(core, tokens)]


def share_out(keep_ref, got_ref, *shares):
    rows = shares[0].shape[0]
    for n, share in enumerate(shares):
        place = part_of(behind("x", lax.axis_size("x") - n), rows) if len(shares) > 1 else slice(None)
        share[...] = keep_ref[place, :] + got_ref[place, :]


def collect(axis, *refs):
    *blocks, out_ref = refs
    rows = blocks[0].shape[0]
    for n, block in enumerate(blocks):
        out_ref[part_of(behind(axis, n), rows), :] = block[...]


def attend(blocks, lens_ref, states, matrix, *refs):
    qk_refs = refs[:blocks]
    out_ref, weights_ref, q_all, k_all = refs[blocks:]
    rows = qk_refs[0].shape[0] // 2
    for n, ref in enumerate(qk_refs):
        q_all[n * rows : (n + 1) * rows, :] = ref[:rows]
        k_all[n * rows : (n + 1) * rows, :] = ref[rows:]
    sequences = lens_ref.shape[0]
    width = q_all.shape[1] // sequences
    for s in range(sequences):
        tokens = slice(s * width, (s + 1) * width)
        scores = dot00(k_all[:, tokens], q_all[:, tokens]) * DK ** (-0.5)
        position = lax.broadcasted_iota(jnp.int32, scores.shape, 0)
        scores = jnp.where(position < lens_ref[s], scores, FLOOR)
        raised = jnp.exp(scores - jnp.max(scores, axis=0, keepdims=True))
        weights_ref[s] = (raised / jnp.sum(raised, axis=0, keepdims=True)).astype(BF16)
    per_core = sequences // CORES
    rows, cols = states.shape[0] // CORES, out_ref.shape[0]
    for n in range(per_core):
        s = lax.axis_index("core") * per_core + n
        aligned = dot10(states[:, part_of(s, width)], weights_ref[s]).astype(BF16)
        total = sum(
            dot10(matrix[c * cols : (c + 1) * cols, :], aligned[c * rows : (c + 1) * rows])
            for c in range(CORES)
        )
        out_ref[:, n * width : (n + 1) * width] = total


def log_total(logits):
    highest = jnp.max(logits, axis=1, keepdims=True)
    raised = jnp.exp(logits - highest)
    summed = jnp.sum(raised, axis=1, keepdims=True)
    return raised, summed, highest + jnp.log(summed)


def target_column(ref, base):
    row = jnp.broadcast_to((ref[...] - base).astype(F32), (STATS, ref.shape[1]))
    return jnp.transpose(row)[:, 0:1].astype(jnp.int32)


def pick(logits, columns):
    lane = lax.broadcasted_iota(jnp.int32, logits.shape, 1)
    return jnp.sum(jnp.where(lane == columns, logits, 0.0), axis=1, keepdims=True)


def pack_columns(columns):
    lane = lax.broadcasted_iota(jnp.int32, (columns[0].shape[0], 128), 1)
    packed = jnp.zeros(lane.shape, F32)
    for k, column in enumerate(columns):
        packed = jnp.where(lane == k, column, packed)
    return packed


def own_student(targets, own_s, mate_s, *refs):
    *chips, head, out_ref, notes_ref, s_all, sems = refs
    rows = own_s.shape[0]
    copies = fetch(sems, (own_s, s_all.at[part_of(block_place(0), rows), :]))
    s_all[part_of(block_place(1), rows), :] = mate_s[...]
    for n, chip in enumerate(chips):
        s_all[part_of(behind("x", n + 1), CORES * rows), :] = chip[...]
    for copy in copies:
        copy.wait()
    logits = dot00(s_all[...], head[...])
    out_ref[...] = logits
    columns = target_column(targets, vocab_base(head.shape[1]))
    _, _, total = log_total(logits)
    notes_ref[...] = pack_columns((total, pick(logits, columns)))


def own_teacher(weights_ref, *refs):
    *chips, head, own_ref, t_all = refs
    sequences, width, _ = weights_ref.shape
    rows = chips[0].shape[0]
    for n, chip in enumerate(chips):
        for s in range(sequences):
            tokens = slice(s * width, (s + 1) * width)
            aligned = dot10(chip[:, tokens], weights_ref[s]).astype(BF16)
            t_all[part_of(behind("x", n), rows), tokens] = aligned
    own_ref[...] = dot00(t_all[...], head[...])


def mapped_teacher(targets, own_ref, *refs):
    *shares, head, mapped_ref, stats_ref, t_all = refs
    parts, blocks = len(shares), lax.axis_size("sv")
    width = shares[0].shape[1]
    rows = shares[0].shape[0] // (CORES * blocks)
    for n, share in enumerate(shares):
        part = behind("x", n) if parts > 1 else 0
        for c in range(CORES):
            tokens = slice(c * width, (c + 1) * width)
            for z in range(blocks):
                place = (c * blocks + z) * rows
                t_all[part_of(z * parts + part, rows), tokens] = share[place : place + rows, :]
    mapped = dot00(t_all[...], head[...])
    mapped_ref[...] = mapped
    own = own_ref[...]
    columns = target_column(targets, vocab_base(head.shape[1]))
    raised, summed, own_total = log_total(own)
    _, _, mapped_total = log_total(mapped)
    spread = jnp.sum(raised * (own - mapped), axis=1, keepdims=True) / summed
    zero = jnp.zeros_like(spread)
    columns = (zero, zero, own_total, mapped_total, zero, zero, spread, pick(mapped, columns))
    stats_ref[...] = jnp.transpose(pack_columns(columns))[:STATS]


def student_side(targets, t_stats, own_ref, notes_ref, halves, head, mapped_ref, stats_ref):
    rows = halves.shape[0] // CORES
    states = jnp.concatenate([halves[:rows], halves[rows:]], axis=1)
    mapped = dot00(states, head[...])
    mapped_ref[...] = mapped
    columns = target_column(targets, vocab_base(head.shape[1]))
    raised, summed, total = log_total(mapped)
    spread = jnp.sum(raised * (mapped - own_ref[...]), axis=1, keepdims=True) / summed
    zero = jnp.zeros_like(spread)
    picked = notes_ref[:, 1:2] + pick(mapped, columns)
    columns = (notes_ref[:, 0:1], total, zero, zero, spread, picked)
    stats_ref[...] = jnp.transpose(pack_columns(columns))[:STATS] + t_stats[...]


def merge_stats(parts):
    highest = parts[0]
    for part in parts[1:]:
        highest = jnp.maximum(highest, part)
    total = highest + jnp.log(sum(jnp.exp(part - highest) for part in parts))
    shares = [jnp.exp(part - total) for part in parts]
    s_spread = sum(share[1:2] * part[4:5] for share, part in zip(shares, parts))
    s_picked = sum(part[5:6] for part in parts)
    t_spread = sum(share[2:3] * part[6:7] for share, part in zip(shares, parts))
    t_picked = sum(part[7:8] for part in parts)
    return total, s_spread, s_picked, t_spread, t_picked


def merge_kernel(*refs):
    *parts, out_ref = refs
    total, *rest = merge_stats([part[...] for part in parts])
    row = lax.broadcasted_iota(jnp.int32, total.shape, 0)
    for k, value in enumerate(rest):
        total = jnp.where(row == 4 + k, value, total)
    out_ref[...] = total


def finish(parts, lens_ref, s_targets, t_targets, so_ref, sm_ref, to_ref, tm_ref, *refs):
    outs, (s_loss, t_loss, s_grad, t_grad), sems = refs[parts : parts + 4], refs[parts + 4 : parts + 8], refs[-1]
    totals, s_spread, s_picked, t_spread, t_picked = merge_stats([ref[...] for ref in refs[:parts]])
    so, sm, to, tm = (totals[k : k + 1] for k in range(4))
    rows = s_loss.shape[1]
    sequences = lens_ref.shape[0]
    width = rows // sequences

    place = lax.broadcasted_iota(jnp.int32, (1, rows), 1)
    live = jnp.zeros((1, rows), jnp.bool_)
    for s in range(sequences):
        live |= (place >= s * width) & (place < s * width + lens_ref[s])
    live = live.astype(F32)
    s_loss[...] = live * (so + sm - s_picked + (s_spread - sm + so))
    t_loss[...] = live * ((t_spread - to + tm) + tm - t_picked)
    copies = fetch(sems, (s_loss, outs[0]), (t_loss, outs[1]))
    base = vocab_base(so_ref.shape[1])
    row = lax.broadcasted_iota(jnp.int32, totals.shape, 0)
    wanted = totals
    for k, value in ((4, live), (5, s_targets[...] - base), (6, t_targets[...] - base)):
        wanted = jnp.where(row == k, value.astype(F32), wanted)
    turned = jnp.transpose(wanted)
    live = turned[:, 4:5]
    lane = lax.broadcasted_iota(jnp.int32, so_ref.shape, 1)
    hot = jnp.where(lane == turned[:, 5:6].astype(jnp.int32), 1.0, 0.0)
    own, mapped = jnp.exp(so_ref[...] - turned[:, 0:1]), jnp.exp(sm_ref[...] - turned[:, 1:2])
    s_grad[...] = (live * (2.0 * own - hot - mapped)).astype(BF16)
    copies += fetch(sems.at[pl.ds(2, 1)], (s_grad, outs[2]))
    hot = jnp.where(lane == turned[:, 6:7].astype(jnp.int32), 1.0, 0.0)
    own, mapped = jnp.exp(to_ref[...] - turned[:, 2:3]), jnp.exp(tm_ref[...] - turned[:, 3:4])
    t_grad[...] = (live * (2.0 * mapped - own - hot)).astype(BF16)
    copies += fetch(sems.at[pl.ds(3, 1)], (t_grad, outs[3]))
    for copy in copies:
        copy.wait()


def after(values, *needs):
    return lax.optimization_barrier((tuple(values), needs))[0]


def body(
    student_states,
    teacher_states,
    student_queries,
    teacher_keys,
    student_targets,
    teacher_targets,
    student_lengths,
    teacher_lengths,
    to_teacher,
    to_student,
    student_head,
    teacher_head,
):
    rows = student_states.shape[0]
    chips, sv_count = lax.axis_size("x"), lax.axis_size("sv")
    vocab = student_head.shape[1]
    tokens = rows // CORES
    sequences = teacher_lengths.shape[0]
    width = rows // sequences
    dma = pltpu.SemaphoreType.DMA

    def both(a):
        return lax.all_gather(a, "core", axis=0, tiled=True)

    def swap(a):
        return lax.ppermute(a, "core", [(0, 1), (1, 0)])

    def shift(a, axis, n):
        count = lax.axis_size(axis)
        return lax.ppermute(a, axis, [(i, (i + n) % count) for i in range(count)])

    def around(a, axis):
        return [shift(a, axis, n) for n in range(1, lax.axis_size(axis))]

    def cross(a, n):
        pairs = [(2 * i + c, (2 * (i + n) + 1 - c) % (CORES * chips)) for i in range(chips) for c in range(CORES)]
        return lax.ppermute(a, ("x", "core"), pairs)

    s_t, t_t = student_states.T, teacher_states.T
    w_t, w_s = to_teacher, to_student.T
    s_targets, t_targets = student_targets.reshape(1, rows), teacher_targets.reshape(1, rows)

    qk, keep, give = kernel_call(
        prepare,
        [shape((2 * student_queries.shape[1], rows), BF16)] + [shape((w_t.shape[1], tokens))] * 2,
        [HBM] * 4,
        [pltpu.VMEM(a.shape, BF16) for a in (s_t, w_t)]
        + [pltpu.VMEM((w_t.shape[1], rows), F32), dma((4,))],
        limit=60,
    )(student_queries.T, teacher_keys.T, s_t, w_t)
    got = swap(give)
    qk_blocks = [qk] + around(qk, "x") + [cross(qk, n) for n in range(chips)]
    split = chips if w_t.shape[1] % (16 * chips) == 0 else 1
    parts_t = kernel_call(
        share_out, [shape((w_t.shape[1] // split, tokens))] * split, [VMEM] * 2
    )(keep, got)

    s_out, t_out, w_out, *parts_t = lax.optimization_barrier((s_t, t_t, w_s, *parts_t))
    other_t = [shift(parts_t[n % split], "x", n) for n in range(1, chips)]
    chip_w_s, chip_t = both(w_out), both(t_out)
    mate_s = swap(s_out)
    far_s = around(after((s_t,), chip_t, chip_w_s)[0], "x")
    features = student_queries.shape[1] * chips * CORES
    part_s, weights = kernel_call(
        functools.partial(attend, len(qk_blocks)),
        (shape((w_s.shape[0], tokens)), shape((sequences, width, width), BF16)),
        [SMEM] + [VMEM] * (2 + len(qk_blocks)),
        [pltpu.VMEM((features, rows), BF16)] * 2,
    )(teacher_lengths, chip_t, chip_w_s, *qk_blocks)

    own_part, *other_t, part_s, mate_s = lax.optimization_barrier(
        (parts_t[0], *other_t, part_s, mate_s)
    )
    into_t = functools.reduce(jnp.add, other_t, own_part).astype(BF16)
    into_t = [into_t] + around(into_t, "sv")
    other_s = around(part_s, "x")
    far_t = around(after((t_t,), *other_t)[0], "x")
    s_blocks = [both(a) for a in after(far_s, *other_t)]

    logits = shape((rows, vocab))
    s_own, s_notes = kernel_call(
        own_student,
        (logits, shape((rows, 128))),
        [VMEM, HBM] + [VMEM] * (2 + len(s_blocks)),
        [pltpu.VMEM((student_head.shape[0], rows), BF16), dma((1,))],
    )(s_targets, s_t, mate_s, *s_blocks, student_head)

    *into_t, part_s, other_s, s_own = lax.optimization_barrier((*into_t, part_s, other_s, s_own))
    into_t = kernel_call(
        functools.partial(collect, "sv"),
        shape((sv_count * into_t[0].shape[0], tokens), BF16),
        [VMEM] * sv_count,
    )(*into_t)
    into_t, part_s = lax.optimization_barrier((into_t, part_s))
    into_s = functools.reduce(jnp.add, other_s, part_s).astype(BF16)
    into_s = [into_s] + around(into_s, "sv")
    t_shares = [into_t] + (around(into_t, "x") if split > 1 else [])
    t_shares = [both(a) for a in t_shares]
    t_blocks = [chip_t] + [both(a) for a in far_t]
    t_own = kernel_call(
        own_teacher,
        logits,
        [VMEM] * (2 + len(t_blocks)),
        [pltpu.VMEM((teacher_head.shape[0], rows), BF16)],
    )(weights, *t_blocks, teacher_head)
    t_mapped, t_stats = kernel_call(
        mapped_teacher,
        (logits, shape((STATS, rows))),
        [VMEM] * (3 + len(t_shares)),
        [pltpu.VMEM((teacher_head.shape[0], rows), BF16)],
    )(t_targets, t_own, *t_shares, teacher_head)

    into_s = kernel_call(
        functools.partial(collect, "sv"),
        shape((sv_count * into_s[0].shape[0], tokens), BF16),
        [VMEM] * sv_count,
    )(*after(into_s, t_stats))
    s_mapped, stats = kernel_call(
        student_side, (logits, shape((STATS, rows))), [VMEM] * 6
    )(s_targets, t_stats, s_own, s_notes, both(into_s), student_head)

    stats = [stats] + around(stats, "x") + [cross(stats, n) for n in range(chips)]
    stats = kernel_call(merge_kernel, shape((STATS, rows)), [VMEM] * len(stats))(*stats)
    stats = [stats] + around(stats, "sv")
    s_loss, t_loss, s_grad, t_grad = kernel_call(
        functools.partial(finish, sv_count),
        (shape((1, rows)), shape((1, rows)), shape((rows, vocab), BF16), shape((rows, vocab), BF16)),
        [SMEM] + [VMEM] * (6 + sv_count),
        [pltpu.VMEM((1, rows), F32)] * 2 + [pltpu.VMEM((rows, vocab), BF16)] * 2 + [dma((4,))],
        outs=HBM,
    )(student_lengths, s_targets, t_targets, s_own, s_mapped, t_own, t_mapped, *stats)
    return s_loss.reshape(rows), t_loss.reshape(rows), s_grad, t_grad


def solution(mesh):
    grp, sv, tv = (mesh.shape[name] for name in ("grp", "sv", "tv"))
    devices = mesh.devices.reshape(grp, sv, tv // CORES, CORES)
    mesh = jax.sharding.Mesh(devices, ("grp", "sv", "x", "core"))
    tv = ("x", "core")
    columns = ("sv", "x", "core")
    in_specs = (P("grp", tv),) * 4 + (P("grp"),) * 4
    in_specs += (P(tv, "sv"),) * 2 + (P(None, columns),) * 2
    out_specs = (P("grp"), P("grp"), P("grp", columns), P("grp", columns))
    return jax.shard_map(body, mesh=mesh, in_specs=in_specs, out_specs=out_specs, check_vma=False)
```

```python
import functools

import jax
import jax.numpy as jnp
from jax import lax
from jax.experimental import pallas as pl
from jax.experimental.pallas import tpu as pltpu
from jax.sharding import PartitionSpec as P

DK = 256
FLOOR = -1e30
CORES = 2
STATS = 8
F32 = jnp.float32
BF16 = jnp.bfloat16

VMEM = pl.BlockSpec(memory_space=pltpu.VMEM)
SMEM = pl.BlockSpec(memory_space=pltpu.SMEM)
HBM = pl.BlockSpec(memory_space=pltpu.HBM)


def shape(dims, dtype=F32):
    return jax.ShapeDtypeStruct(dims, dtype)


def kernel_call(body, out_shape, in_specs, scratch=(), limit=32, outs=VMEM):
    single = not isinstance(out_shape, (tuple, list))
    return pl.pallas_call(
        body,
        out_shape=out_shape,
        in_specs=in_specs,
        out_specs=outs if single else [outs] * len(out_shape),
        scratch_shapes=list(scratch),
        compiler_params=pltpu.CompilerParams(vmem_limit_bytes=limit * 2**20),

    )


def dot00(a, b):
    return lax.dot_general(a, b, (((0,), (0,)), ((), ())), preferred_element_type=F32)


def dot10(a, b):
    return lax.dot_general(a, b, (((1,), (0,)), ((), ())), preferred_element_type=F32)


def part_of(index, width):
    return pl.ds(pl.multiple_of(index * width, width), width)


def behind(axis, offset):
    count = lax.axis_size(axis)
    return lax.rem(lax.axis_index(axis) - offset + count, count)


def block_place(n):
    core = lax.axis_index("core")
    return behind("x", n // CORES) * CORES + (core if n % CORES == 0 else 1 - core)


def vocab_base(vocab):
    place = lax.axis_index("sv") * lax.axis_size("x") + lax.axis_index("x")
    return (place * CORES + lax.axis_index("core")) * vocab


def fetch(sems, *pairs):
    copies = [pltpu.make_async_copy(a, b, sems.at[n]) for n, (a, b) in enumerate(pairs)]
    for copy in copies:
        copy.start()
    return copies


def prepare(q_ref, k_ref, own_s, own_w, qk_ref, keep_ref, give_ref, s_v, w_v, total, sems):
    rows = q_ref.shape[0]
    qk_pairs = (q_ref, qk_ref.at[:rows]), (k_ref, qk_ref.at[rows:])
    copies = fetch(sems, (own_s, s_v), (own_w, w_v), *qk_pairs)
    for copy in copies:
        copy.wait()
    core = lax.axis_index("core")
    tokens = keep_ref.shape[1]
    total[...] = dot00(w_v[...], s_v[...])
    give_ref[...] = total[:, part_of(1 - core, tokens)]
    keep_ref[...] = total[:, part_of(core, tokens)]


def share_out(keep_ref, got_ref, *shares):
    rows = shares[0].shape[0]
    for n, share in enumerate(shares):
        place = part_of(behind("x", lax.axis_size("x") - n), rows) if len(shares) > 1 else slice(None)
        share[...] = keep_ref[place, :] + got_ref[place, :]


def pairs_up(count):
    return count & (count - 1) == 0


def collect(axis, paired, *refs):
    *blocks, out_ref = refs
    rows = blocks[0].shape[0]
    for n, block in enumerate(blocks):
        index = lax.axis_index(axis) ^ n if paired else behind(axis, n)
        out_ref[part_of(index, rows), :] = block[...]


def attend(blocks, lens_ref, states, matrix, *refs):
    qk_refs = refs[:blocks]
    out_ref, weights_ref, q_all, k_all = refs[blocks:]
    rows = qk_refs[0].shape[0] // 2
    for n, ref in enumerate(qk_refs):
        q_all[n * rows : (n + 1) * rows, :] = ref[:rows]
        k_all[n * rows : (n + 1) * rows, :] = ref[rows:]
    sequences = lens_ref.shape[0]
    width = q_all.shape[1] // sequences
    for s in range(sequences):
        tokens = slice(s * width, (s + 1) * width)
        scores = dot00(k_all[:, tokens], q_all[:, tokens]) * DK ** (-0.5)
        position = lax.broadcasted_iota(jnp.int32, scores.shape, 0)
        scores = jnp.where(position < lens_ref[s], scores, FLOOR)
        raised = jnp.exp(scores - jnp.max(scores, axis=0, keepdims=True))
        weights_ref[s] = (raised / jnp.sum(raised, axis=0, keepdims=True)).astype(BF16)
    per_core = sequences // CORES
    rows, cols = states.shape[0] // CORES, out_ref.shape[0]
    for n in range(per_core):
        s = lax.axis_index("core") * per_core + n
        aligned = dot10(states[:, part_of(s, width)], weights_ref[s]).astype(BF16)
        total = sum(
            dot10(matrix[c * cols : (c + 1) * cols, :], aligned[c * rows : (c + 1) * rows])
            for c in range(CORES)
        )
        out_ref[:, n * width : (n + 1) * width] = total


def log_total(logits):
    highest = jnp.max(logits, axis=1, keepdims=True)
    raised = jnp.exp(logits - highest)
    summed = jnp.sum(raised, axis=1, keepdims=True)
    return raised, summed, highest + jnp.log(summed)


def target_column(ref, base):
    row = jnp.broadcast_to((ref[...] - base).astype(F32), (STATS, ref.shape[1]))
    return jnp.transpose(row)[:, 0:1].astype(jnp.int32)


def pick(logits, columns):
    lane = lax.broadcasted_iota(jnp.int32, logits.shape, 1)
    return jnp.sum(jnp.where(lane == columns, logits, 0.0), axis=1, keepdims=True)


def pack_columns(columns):
    lane = lax.broadcasted_iota(jnp.int32, (columns[0].shape[0], 128), 1)
    packed = jnp.zeros(lane.shape, F32)
    for k, column in enumerate(columns):
        packed = jnp.where(lane == k, column, packed)
    return packed


def own_student(targets, own_s, mate_s, *refs):
    *chips, head, out_ref, notes_ref, s_all, sems = refs
    rows = own_s.shape[0]
    copies = fetch(sems, (own_s, s_all.at[part_of(block_place(0), rows), :]))
    s_all[part_of(block_place(1), rows), :] = mate_s[...]
    for n, chip in enumerate(chips):
        s_all[part_of(behind("x", n + 1), CORES * rows), :] = chip[...]
    for copy in copies:
        copy.wait()
    logits = dot00(s_all[...], head[...])
    out_ref[...] = logits
    columns = target_column(targets, vocab_base(head.shape[1]))
    _, _, total = log_total(logits)
    notes_ref[...] = pack_columns((total, pick(logits, columns)))


def own_teacher(weights_ref, *refs):
    *chips, head, own_ref, t_all = refs
    sequences, width, _ = weights_ref.shape
    rows = chips[0].shape[0]
    for n, chip in enumerate(chips):
        for s in range(sequences):
            tokens = slice(s * width, (s + 1) * width)
            aligned = dot10(chip[:, tokens], weights_ref[s]).astype(BF16)
            t_all[part_of(behind("x", n), rows), tokens] = aligned
    own_ref[...] = dot00(t_all[...], head[...])


def mapped_teacher(targets, own_ref, *refs):
    *shares, head, mapped_ref, stats_ref, t_all = refs
    parts, blocks = len(shares), lax.axis_size("sv")
    width = shares[0].shape[1]
    rows = shares[0].shape[0] // (CORES * blocks)
    for n, share in enumerate(shares):
        part = behind("x", n) if parts > 1 else 0
        for c in range(CORES):
            tokens = slice(c * width, (c + 1) * width)
            for z in range(blocks):
                place = (c * blocks + z) * rows
                t_all[part_of(z * parts + part, rows), tokens] = share[place : place + rows, :]
    mapped = dot00(t_all[...], head[...])
    mapped_ref[...] = mapped
    own = own_ref[...]
    columns = target_column(targets, vocab_base(head.shape[1]))
    raised, summed, own_total = log_total(own)
    _, _, mapped_total = log_total(mapped)
    spread = jnp.sum(raised * (own - mapped), axis=1, keepdims=True) / summed
    zero = jnp.zeros_like(spread)
    columns = (zero, zero, own_total, mapped_total, zero, zero, spread, pick(mapped, columns))
    stats_ref[...] = jnp.transpose(pack_columns(columns))[:STATS]


def student_side(targets, t_stats, own_ref, notes_ref, halves, head, mapped_ref, stats_ref):
    rows = halves.shape[0] // CORES
    states = jnp.concatenate([halves[:rows], halves[rows:]], axis=1)
    mapped = dot00(states, head[...])
    mapped_ref[...] = mapped
    columns = target_column(targets, vocab_base(head.shape[1]))
    raised, summed, total = log_total(mapped)
    spread = jnp.sum(raised * (mapped - own_ref[...]), axis=1, keepdims=True) / summed
    zero = jnp.zeros_like(spread)
    picked = notes_ref[:, 1:2] + pick(mapped, columns)
    columns = (notes_ref[:, 0:1], total, zero, zero, spread, picked)
    stats_ref[...] = jnp.transpose(pack_columns(columns))[:STATS] + t_stats[...]


def merge_stats(parts):
    highest = parts[0]
    for part in parts[1:]:
        highest = jnp.maximum(highest, part)
    total = highest + jnp.log(sum(jnp.exp(part - highest) for part in parts))
    shares = [jnp.exp(part - total) for part in parts]
    s_spread = sum(share[1:2] * part[4:5] for share, part in zip(shares, parts))
    s_picked = sum(part[5:6] for part in parts)
    t_spread = sum(share[2:3] * part[6:7] for share, part in zip(shares, parts))
    t_picked = sum(part[7:8] for part in parts)
    return total, s_spread, s_picked, t_spread, t_picked


def merge_kernel(*refs):
    *parts, out_ref = refs
    total, *rest = merge_stats([part[...] for part in parts])
    row = lax.broadcasted_iota(jnp.int32, total.shape, 0)
    for k, value in enumerate(rest):
        total = jnp.where(row == 4 + k, value, total)
    out_ref[...] = total


def finish(parts, lens_ref, s_targets, t_targets, so_ref, sm_ref, to_ref, tm_ref, *refs):
    outs, (s_loss, t_loss, s_grad, t_grad), sems = refs[parts : parts + 4], refs[parts + 4 : parts + 8], refs[-1]
    totals, s_spread, s_picked, t_spread, t_picked = merge_stats([ref[...] for ref in refs[:parts]])
    so, sm, to, tm = (totals[k : k + 1] for k in range(4))
    rows = s_loss.shape[1]
    sequences = lens_ref.shape[0]
    width = rows // sequences

    place = lax.broadcasted_iota(jnp.int32, (1, rows), 1)
    live = jnp.zeros((1, rows), jnp.bool_)
    for s in range(sequences):
        live |= (place >= s * width) & (place < s * width + lens_ref[s])
    live = live.astype(F32)
    s_loss[...] = live * (so + sm - s_picked + (s_spread - sm + so))
    t_loss[...] = live * ((t_spread - to + tm) + tm - t_picked)
    copies = fetch(sems, (s_loss, outs[0]), (t_loss, outs[1]))
    base = vocab_base(so_ref.shape[1])
    row = lax.broadcasted_iota(jnp.int32, totals.shape, 0)
    wanted = totals
    for k, value in ((4, live), (5, s_targets[...] - base), (6, t_targets[...] - base)):
        wanted = jnp.where(row == k, value.astype(F32), wanted)
    turned = jnp.transpose(wanted)
    live = turned[:, 4:5]
    lane = lax.broadcasted_iota(jnp.int32, so_ref.shape, 1)
    hot = jnp.where(lane == turned[:, 5:6].astype(jnp.int32), 1.0, 0.0)
    own, mapped = jnp.exp(so_ref[...] - turned[:, 0:1]), jnp.exp(sm_ref[...] - turned[:, 1:2])
    s_grad[...] = (live * (2.0 * own - hot - mapped)).astype(BF16)
    copies += fetch(sems.at[pl.ds(2, 1)], (s_grad, outs[2]))
    hot = jnp.where(lane == turned[:, 6:7].astype(jnp.int32), 1.0, 0.0)
    own, mapped = jnp.exp(to_ref[...] - turned[:, 2:3]), jnp.exp(tm_ref[...] - turned[:, 3:4])
    t_grad[...] = (live * (2.0 * mapped - own - hot)).astype(BF16)
    copies += fetch(sems.at[pl.ds(3, 1)], (t_grad, outs[3]))
    for copy in copies:
        copy.wait()


def after(values, *needs):
    return lax.optimization_barrier((tuple(values), needs))[0]


def body(
    student_states,
    teacher_states,
    student_queries,
    teacher_keys,
    student_targets,
    teacher_targets,
    student_lengths,
    teacher_lengths,
    to_teacher,
    to_student,
    student_head,
    teacher_head,
):
    rows = student_states.shape[0]
    chips, sv_count = lax.axis_size("x"), lax.axis_size("sv")
    vocab = student_head.shape[1]
    tokens = rows // CORES
    sequences = teacher_lengths.shape[0]
    width = rows // sequences
    dma = pltpu.SemaphoreType.DMA

    def both(a):
        return lax.all_gather(a, "core", axis=0, tiled=True)

    def swap(a):
        return lax.ppermute(a, "core", [(0, 1), (1, 0)])

    def shift(a, axis, n):
        count = lax.axis_size(axis)
        return lax.ppermute(a, axis, [(i, (i + n) % count) for i in range(count)])

    def around(a, axis):
        return [shift(a, axis, n) for n in range(1, lax.axis_size(axis))]

    def exchange(a, axis):
        count = lax.axis_size(axis)
        return [lax.ppermute(a, axis, [(i, i ^ n) for i in range(count)]) for n in range(1, count)]

    def cross(a, n):
        pairs = [(2 * i + c, (2 * (i + n) + 1 - c) % (CORES * chips)) for i in range(chips) for c in range(CORES)]
        return lax.ppermute(a, ("x", "core"), pairs)

    s_t, t_t = student_states.T, teacher_states.T
    w_t, w_s = to_teacher, to_student.T
    s_targets, t_targets = student_targets.reshape(1, rows), teacher_targets.reshape(1, rows)

    qk, keep, give = kernel_call(
        prepare,
        [shape((2 * student_queries.shape[1], rows), BF16)] + [shape((w_t.shape[1], tokens))] * 2,
        [HBM] * 4,
        [pltpu.VMEM(a.shape, BF16) for a in (s_t, w_t)]
        + [pltpu.VMEM((w_t.shape[1], rows), F32), dma((4,))],
        limit=60,
    )(student_queries.T, teacher_keys.T, s_t, w_t)
    got = swap(give)
    qk_blocks = [qk] + around(qk, "x") + [cross(qk, n) for n in range(chips)]
    split = chips if w_t.shape[1] % (16 * chips) == 0 else 1
    parts_t = kernel_call(
        share_out, [shape((w_t.shape[1] // split, tokens))] * split, [VMEM] * 2
    )(keep, got)

    s_out, t_out, w_out, *parts_t = lax.optimization_barrier((s_t, t_t, w_s, *parts_t))
    other_t = [shift(parts_t[n % split], "x", n) for n in range(1, chips)]
    chip_w_s, chip_t = both(w_out), both(t_out)
    mate_s = swap(s_out)
    far_s = around(after((s_t,), chip_t, chip_w_s)[0], "x")
    features = student_queries.shape[1] * chips * CORES
    part_s, weights = kernel_call(
        functools.partial(attend, len(qk_blocks)),
        (shape((w_s.shape[0], tokens)), shape((sequences, width, width), BF16)),
        [SMEM] + [VMEM] * (2 + len(qk_blocks)),
        [pltpu.VMEM((features, rows), BF16)] * 2,
    )(teacher_lengths, chip_t, chip_w_s, *qk_blocks)

    own_part, *other_t, part_s, mate_s = lax.optimization_barrier(
        (parts_t[0], *other_t, part_s, mate_s)
    )
    into_t = functools.reduce(jnp.add, other_t, own_part).astype(BF16)
    into_t = [into_t] + (exchange(into_t, "sv") if pairs_up(sv_count) else around(into_t, "sv"))
    other_s = around(part_s, "x")
    far_t = around(after((t_t,), *other_t)[0], "x")
    s_blocks = [both(a) for a in after(far_s, *other_t)]

    logits = shape((rows, vocab))
    s_own, s_notes = kernel_call(
        own_student,
        (logits, shape((rows, 128))),
        [VMEM, HBM] + [VMEM] * (2 + len(s_blocks)),
        [pltpu.VMEM((student_head.shape[0], rows), BF16), dma((1,))],
    )(s_targets, s_t, mate_s, *s_blocks, student_head)

    *into_t, part_s, other_s, s_own = lax.optimization_barrier((*into_t, part_s, other_s, s_own))
    into_t = kernel_call(
        functools.partial(collect, "sv", pairs_up(sv_count)),
        shape((sv_count * into_t[0].shape[0], tokens), BF16),
        [VMEM] * sv_count,
    )(*into_t)
    into_t, part_s = lax.optimization_barrier((into_t, part_s))
    into_s = functools.reduce(jnp.add, other_s, part_s).astype(BF16)
    into_s = [into_s] + (exchange(into_s, "sv") if pairs_up(sv_count) else around(into_s, "sv"))
    t_shares = [into_t] + (around(into_t, "x") if split > 1 else [])
    t_shares = [both(a) for a in t_shares]
    t_blocks = [chip_t] + [both(a) for a in far_t]
    t_own = kernel_call(
        own_teacher,
        logits,
        [VMEM] * (2 + len(t_blocks)),
        [pltpu.VMEM((teacher_head.shape[0], rows), BF16)],
    )(weights, *t_blocks, teacher_head)
    t_mapped, t_stats = kernel_call(
        mapped_teacher,
        (logits, shape((STATS, rows))),
        [VMEM] * (3 + len(t_shares)),
        [pltpu.VMEM((teacher_head.shape[0], rows), BF16)],
    )(t_targets, t_own, *t_shares, teacher_head)

    into_s = kernel_call(
        functools.partial(collect, "sv", pairs_up(sv_count)),
        shape((sv_count * into_s[0].shape[0], tokens), BF16),
        [VMEM] * sv_count,
    )(*after(into_s, t_stats))
    s_mapped, stats = kernel_call(
        student_side, (logits, shape((STATS, rows))), [VMEM] * 6
    )(s_targets, t_stats, s_own, s_notes, both(into_s), student_head)

    stats = [stats] + around(stats, "x") + [cross(stats, n) for n in range(chips)]
    stats = kernel_call(merge_kernel, shape((STATS, rows)), [VMEM] * len(stats))(*stats)
    stats = [stats] + around(stats, "sv")
    s_loss, t_loss, s_grad, t_grad = kernel_call(
        functools.partial(finish, sv_count),
        (shape((1, rows)), shape((1, rows)), shape((rows, vocab), BF16), shape((rows, vocab), BF16)),
        [SMEM] + [VMEM] * (6 + sv_count),
        [pltpu.VMEM((1, rows), F32)] * 2 + [pltpu.VMEM((rows, vocab), BF16)] * 2 + [dma((4,))],
        outs=HBM,
    )(student_lengths, s_targets, t_targets, s_own, s_mapped, t_own, t_mapped, *stats)
    return s_loss.reshape(rows), t_loss.reshape(rows), s_grad, t_grad


def solution(mesh):
    grp, sv, tv = (mesh.shape[name] for name in ("grp", "sv", "tv"))
    devices = mesh.devices.reshape(grp, sv, tv // CORES, CORES)
    mesh = jax.sharding.Mesh(devices, ("grp", "sv", "x", "core"))
    tv = ("x", "core")
    columns = ("sv", "x", "core")
    in_specs = (P("grp", tv),) * 4 + (P("grp"),) * 4
    in_specs += (P(tv, "sv"),) * 2 + (P(None, columns),) * 2
    out_specs = (P("grp"), P("grp"), P("grp", columns), P("grp", columns))
    return jax.shard_map(body, mesh=mesh, in_specs=in_specs, out_specs=out_specs, check_vma=False)
```
